32 devices in a mesh: groups: 2 (over x), frame: 16 (over z, y, core).
Axes of the slice: x: 2, y: 2, z: 4, core: 2. Of those that a mesh axis runs over, the one named last changes fastest.
Arguments:
- latent_images: bfloat16 [64, 4, 240, 256], P(('groups', 'frame')), parts along dimension 0, may hold values from -6 to 6
- initial_group_scale: float32 [256], replicated, may hold values from 0.1 to 1.9
- initial_conv_taps: bfloat16 [3, 3, 256, 256], replicated, may hold values from -0.125 to 0.125
- later_group_scale: float32 [256], replicated, may hold values from 0.1 to 1.9
- later_conv_taps: bfloat16 [3, 3, 256, 256], replicated, may hold values from -0.125 to 0.125
- prenormal_scale_vector: float32 [256], replicated, may hold values from 0.1 to 1.9
- asking_projection_matrix: bfloat16 [256, 256], replicated, may hold values from -0.375 to 0.375
- matching_projection_matrix: bfloat16 [256, 256], replicated, may hold values from -0.375 to 0.375
- content_projection_matrix: bfloat16 [256, 256], replicated, may hold values from -0.375 to 0.375
- closing_projection_matrix: bfloat16 [256, 256], replicated, may hold values from -0.375 to 0.375
- neighbour_time_taps: bfloat16 [3, 256, 256], replicated, may hold values from -0.21875 to 0.21875
- score_sharpness: float32 [4], replicated, may hold values from 0.5 to 120
Outputs:
- result: bfloat16 [64, 4, 240, 256], P(('groups', 'frame')), parts along dimension 0
The draws below stay inside these ranges and needn't reach their ends.
There are 2 independent parts, one for each index of `groups`. The reference program is written for one: setup_inputs(seed, part) draws one part's arguments, and reference() takes and returns one part's arrays. A program takes and returns all parts, laid end to end along the dimension named above; an argument that names none is the same for every part. Nothing has to cross between parts.
All inputs are finite; a program needn't handle non-finite values.
Results may differ from the reference program's by a relative error of at most 0.022.
The reference program's roundings to bfloat16 on the way count: a program that leaves them out, or rounds other values in their place, can miss the bound.
Values may be sent and summed in bfloat16 or wider, within the bound.
A program may use at most 64 MiB of HBM per device.

```python
import math
import jax
import jax.numpy as jnp
from jax import lax

C = 256
HEADS = 4
GROUPS = 32
HT = 4
W = 240
FRAMES = 32
OWN = 60
N_FRAME = 16


def draw_score_sharpness(key, part):
    logs = jax.random.uniform(key, (HEADS,), jnp.float32, math.log(0.5), math.log(2.0))
    return jnp.exp(logs)


def block_levels(rng, dims, pieces, smallest, top_value):
    loudness, own = 1.0, jax.random.fold_in(rng, 6)
    for dim, shards_of in pieces:
        draws = jnp.exp(jax.random.uniform(jax.random.fold_in(own, dim), (shards_of,), jnp.float32, smallest / len(pieces), top_value / len(pieces)))
        loudness = loudness * jnp.repeat(draws, dims[dim] // shards_of).reshape([-1 if axis == dim else 1 for axis in range(len(dims))])
    return loudness


def centred(stream_key, shape, deviation, limit, shards=(), dtype=jnp.bfloat16):
    loudness = block_levels(stream_key, shape, shards, -0.22, 0.18) if shards else 1.0
    array = jax.random.normal(stream_key, shape, jnp.float32) * deviation * loudness
    return jnp.minimum(jnp.maximum(array, -limit), limit).astype(dtype)


def setup_inputs(seed: int = 0, part: int = 0) -> dict:
    streams_of = jax.random.split(jax.random.key(seed), 13)
    part_keys = jax.random.split(jax.random.fold_in(streams_of[12], part), 13)
    return {
        "latent_images": centred(part_keys[0], (FRAMES, HT, W, C), 1.0, 6.0, ((0, 16),)),
        "initial_group_scale": jnp.clip(1.0 + 0.18 * jax.random.normal(streams_of[1], (C,), jnp.float32), 0.1, 1.9),
        "initial_conv_taps": centred(streams_of[2], (3, 3, C, C), (9 * C) ** -0.5, 0.125),
        "later_group_scale": jnp.clip(1.0 + 0.18 * jax.random.normal(streams_of[3], (C,), jnp.float32), 0.1, 1.9),
        "later_conv_taps": centred(streams_of[4], (3, 3, C, C), (9 * C) ** -0.5, 0.125),
        "prenormal_scale_vector": jnp.clip(1.0 + 0.18 * jax.random.normal(streams_of[5], (C,), jnp.float32), 0.1, 1.9),
        "asking_projection_matrix": centred(streams_of[6], (C, C), C ** -0.5, 0.375),
        "matching_projection_matrix": centred(streams_of[7], (C, C), C ** -0.5, 0.375),
        "content_projection_matrix": centred(streams_of[8], (C, C), C ** -0.5, 0.375),
        "closing_projection_matrix": centred(streams_of[9], (C, C), C ** -0.5, 0.375),
        "neighbour_time_taps": centred(streams_of[10], (3, C, C), (3 * C) ** -0.5, 0.21875),
        "score_sharpness": draw_score_sharpness(jax.random.fold_in(streams_of[12], 71), part),
    }


EPSILON = 1e-05

def group_norm(values, gain):
    input_shape = values.shape
    grouped = values.reshape(input_shape[:-1] + (GROUPS, input_shape[-1] // GROUPS))
    average = lax.optimization_barrier(jnp.mean(grouped, axis=(1, 2, 4), keepdims=True))
    centered = grouped - average
    spread = lax.optimization_barrier(jnp.mean(centered * centered, axis=(1, 2, 4), keepdims=True))
    return (centered * lax.rsqrt(spread + EPSILON)).reshape(input_shape) * gain

def spatial_conv(active, weight):
    height = active.shape[1]
    breadth = active.shape[2]
    channels = active.shape[3]
    padded = jnp.pad(active, ((0, 0), (1, 1), (1, 1), (0, 0)))
    total = jnp.zeros((active.shape[0] * height * breadth, channels), jnp.float32)
    for row_tap in range(3):
        for col_tap in range(3):
            window = padded[:, row_tap:row_tap + height, col_tap:col_tap + breadth, :].reshape(-1, channels)
            total = total + jnp.dot(window, weight[row_tap, col_tap], preferred_element_type=jnp.float32)
    return total.reshape(active.shape)

def spatial_block(latent_images, initial_group_scale, initial_conv_taps, later_group_scale, later_conv_taps):
    first = jax.nn.silu(group_norm(latent_images.astype(jnp.float32), initial_group_scale)).astype(jnp.bfloat16)
    hidden = spatial_conv(first, initial_conv_taps)
    second = jax.nn.silu(group_norm(hidden, later_group_scale)).astype(jnp.bfloat16)
    return (latent_images.astype(jnp.float32) + spatial_conv(second, later_conv_taps)).astype(jnp.bfloat16)

def across_time_mixing(upscaling_unit_step, prenormal_scale_vector, asking_projection_matrix, matching_projection_matrix, content_projection_matrix, closing_projection_matrix, score_sharpness):
    count, pixels, channels = upscaling_unit_step.shape
    number_of_subspaces = score_sharpness.shape[0]
    subspace_dimension = channels // number_of_subspaces
    widened = upscaling_unit_step.astype(jnp.float32)
    average = lax.optimization_barrier(jnp.mean(widened, axis=-1, keepdims=True))
    centered = widened - average
    spread = lax.optimization_barrier(jnp.mean(centered * centered, axis=-1, keepdims=True))
    normed = (centered * lax.rsqrt(spread + EPSILON) * prenormal_scale_vector).astype(jnp.bfloat16).reshape(-1, channels)

    def project(weight):
        return jnp.dot(normed, weight, preferred_element_type=jnp.float32).astype(jnp.bfloat16).reshape(count, pixels, number_of_subspaces, subspace_dimension)
    queries = project(asking_projection_matrix)
    keys = project(matching_projection_matrix)
    values = project(content_projection_matrix)
    raw_pair_scores = jnp.einsum('fphd,gphd->phfg', queries.astype(jnp.float32), keys.astype(jnp.float32))
    raw_pair_scores = raw_pair_scores * (score_sharpness / math.sqrt(subspace_dimension))[None, :, None, None]
    probs = jax.nn.softmax(raw_pair_scores, axis=-1).astype(jnp.bfloat16)
    attended = jnp.einsum('phfg,gphd->fphd', probs.astype(jnp.float32), values.astype(jnp.float32))
    attended = attended.astype(jnp.bfloat16).reshape(-1, channels)
    output = widened + jnp.dot(attended, closing_projection_matrix, preferred_element_type=jnp.float32).reshape(upscaling_unit_step.shape)
    return output.astype(jnp.bfloat16)

def time_mix(padded, weight):
    count = padded.shape[0] - 2
    channels = padded.shape[-1]
    center = padded[1:count + 1]
    total = center.astype(jnp.float32).reshape(-1, channels)
    for offset in range(3):
        total = total + jnp.dot(padded[offset:offset + count].reshape(-1, channels), weight[offset], preferred_element_type=jnp.float32)
    return total.reshape(center.shape).astype(jnp.bfloat16)

def reference(latent_images, initial_group_scale, initial_conv_taps, later_group_scale, later_conv_taps, prenormal_scale_vector, asking_projection_matrix, matching_projection_matrix, content_projection_matrix, closing_projection_matrix, neighbour_time_taps, score_sharpness):

    def one_frame(single):
        return spatial_block(single[None], initial_group_scale, initial_conv_taps, later_group_scale, later_conv_taps)[0]
    spatial = lax.map(one_frame, latent_images)
    blocks = spatial.reshape(FRAMES, N_FRAME, OWN, C).transpose(1, 0, 2, 3)

    def owner(upscaling_unit_step):
        mixed_result_tensor = across_time_mixing(upscaling_unit_step, prenormal_scale_vector, asking_projection_matrix, matching_projection_matrix, content_projection_matrix, closing_projection_matrix, score_sharpness)
        return time_mix(jnp.pad(mixed_result_tensor, ((1, 1), (0, 0), (0, 0))), neighbour_time_taps)
    finished = lax.map(owner, blocks)
    return finished.transpose(1, 0, 2, 3).reshape(FRAMES, HT, W, C)
```

```python
import functools
import math

import jax
import jax.numpy as jnp
from jax import lax
from jax.experimental import pallas as pl
from jax.experimental.pallas import tpu as pltpu
from jax.sharding import PartitionSpec as P

GROUPS = 32
EPSILON = 1e-05
SUB = 8
UNIT = 16
F32 = jnp.float32
BF16 = jnp.bfloat16
MESH = pl.DeviceIdType.MESH


def dot(a, b):
    return jnp.dot(a, b, preferred_element_type=F32)


def shares(width, owners):
    units = width // UNIT
    first = [c * units // owners for c in range(owners + 1)]
    return first, [first[c + 1] - first[c] for c in range(owners)]


def cut(most, parts):
    return [most * k // parts for k in range(parts + 1)]


def kernel(
    n,
    per,
    height,
    width,
    heads,
    parts,
    x_hbm,
    g1_hbm,
    w1_hbm,
    g2_hbm,
    w2_hbm,
    pn_hbm,
    wq_hbm,
    wk_hbm,
    wv_hbm,
    wo_hbm,
    tt_hbm,
    sharp_hbm,
    out_ref,
    x_ref,
    g1_ref,
    w1_ref,
    g2_ref,
    w2_ref,
    pn_ref,
    wq_ref,
    wk_ref,
    wv_ref,
    wo_ref,
    tt_ref,
    sharp_ref,
    act,
    hid,
    local,
    recv,
    q_s,
    k_s,
    v_s,
    o_s,
    fin,
    load,
    send1,
    recv1,
    send2,
    recv2,
):
    me = lax.axis_index("frame")
    pixels = height * width
    channels = x_ref.shape[-1]
    frames = n * per
    owners = n // height
    units = width // UNIT
    first, counts = shares(width, owners)
    most = max(counts)
    rows = frames * SUB
    block = min(rows, 256)
    halves = UNIT // SUB
    plane = me // owners
    seat = me % owners
    order = [
        height - 1 - plane,
        lax.rem(plane + height // 2, height),
        plane + 1 - 2 * lax.rem(plane, 2),
        plane,
    ]

    def pieces(f, c):
        cuts = cut(most, parts) if f == per - 1 else [0, most]
        return [
            (k, cuts[k], min(cuts[k + 1], counts[c]))
            for k in range(len(cuts) - 1)
            if cuts[k] < counts[c]
        ]

    def peer(j):
        return lax.rem(me + j, n), lax.rem(me + n - j, n)

    loads = []
    for source, target in (
        (x_hbm.at[0], x_ref.at[0]),
        (g1_hbm, g1_ref),
        (w1_hbm, w1_ref),
        (g2_hbm, g2_ref),
        (w2_hbm, w2_ref),
        *((x_hbm.at[f], x_ref.at[f]) for f in range(1, per)),
        (pn_hbm, pn_ref),
        (wq_hbm, wq_ref),
        (wk_hbm, wk_ref),
        (wv_hbm, wv_ref),
        (wo_hbm, wo_ref),
        (tt_hbm, tt_ref),
        (sharp_hbm, sharp_ref),
    ):
        loads.append(pltpu.make_async_copy(source, target, load.at[len(loads)]))
    for copy in loads:
        copy.start()

    barrier = pltpu.get_barrier_semaphore()

    @pl.loop(1, n)
    def _(j):
        to, _ = peer(lax.rem(j + n // 2 - 1, n - 1) + 1)
        pl.semaphore_signal(barrier, inc=1, device_id={"frame": to}, device_id_type=MESH)

    act[pl.ds(0, width), :] = jnp.zeros((width, 3 * channels), BF16)
    act[pl.ds((height + 1) * width, width), :] = jnp.zeros((width, 3 * channels), BF16)

    per_group = channels // GROUPS
    lanes = lax.broadcasted_iota(jnp.int32, (8, channels), 1)
    column = lax.broadcasted_iota(jnp.int32, (width, channels), 0)

    def group_mean(values):
        total = jnp.broadcast_to(values, (8, channels))
        step = 1
        while step < per_group:
            total = total + jnp.where(
                (lanes // step) % 2 == 0,
                pltpu.roll(total, channels - step, 1),
                pltpu.roll(total, step, 1),
            )
            step *= 2
        return total[:1] * (1.0 / per_group)

    def fold(v):
        return jnp.sum(v.reshape(width // 8, 8, channels), axis=0)

    def moments(shift, s1, s2):
        m1 = jnp.sum(s1, axis=0, keepdims=True) * (1.0 / pixels)
        m2 = jnp.sum(s2, axis=0, keepdims=True) * (1.0 / pixels)
        own = shift + m1
        mean = group_mean(own)
        off = own - mean
        var = group_mean(jnp.maximum(m2 - m1 * m1, 0.0) + off * off)
        return mean, lax.rsqrt(var + EPSILON)

    def row_of(i):
        return pl.ds(i * width, width)

    def activate(value, mean, inv, gain):
        half = inv * gain * 0.5
        for i in range(height):
            v = (value(i) - mean) * half
            y = (v * jnp.tanh(v) + v).astype(BF16)
            wide = y.astype(F32)
            there = row_of(i + 1)
            act[there, pl.ds(0, channels)] = jnp.where(
                column == 0, 0.0, pltpu.roll(wide, 1, 0)
            ).astype(BF16)
            act[there, pl.ds(channels, channels)] = y
            act[there, pl.ds(2 * channels, channels)] = jnp.where(
                column == width - 1, 0.0, pltpu.roll(wide, width - 1, 0)
            ).astype(BF16)

    def conv(w_ref, start):
        total = None
        for a in range(3):
            term = dot(
                act[pl.ds(start + a * width, width), :],
                w_ref[pl.ds(a * 3 * channels, 3 * channels), :],
            )
            total = term if total is None else total + term
        return total

    def sums(value, shift, s1, s2):
        d = value - shift
        return s1 + fold(d), s2 + fold(d * d)

    def forward(f, k, to, source, start, low, high):
        return pltpu.make_async_remote_copy(
            src_ref=local.at[f, pl.ds(start, (high - low) * UNIT)],
            dst_ref=recv.at[source * per + f, pl.ds(low * UNIT, (high - low) * UNIT)],
            send_sem=send1.at[f, k, to],
            recv_sem=recv1.at[f, k, source],
            device_id={"frame": to},
            device_id_type=MESH,
        )

    zero = jnp.zeros((8, channels), F32)

    for f in range(per):
        if f == 0:
            loads[0].wait()
            loads[1].wait()
        else:
            loads[4 + f].wait()

        def pixels_of(i):
            return x_ref[f, row_of(i), :].astype(F32)

        shift = pixels_of(0)[:1]
        s1, s2 = zero, zero
        for i in range(height):
            s1, s2 = sums(pixels_of(i), shift, s1, s2)
        activate(pixels_of, *moments(shift, s1, s2), g1_ref[...])

        if f == 0:
            loads[2].wait()
        shift, s1, s2 = None, zero, zero
        for i in range(height):
            value = conv(w1_ref, i * width)
            hid[row_of(i), :] = value
            if shift is None:
                shift = value[:1]
            s1, s2 = sums(value, shift, s1, s2)
        if f == 0:
            loads[3].wait()
        activate(lambda i: hid[row_of(i), :], *moments(shift, s1, s2), g2_ref[...])

        if f == 0:
            loads[4].wait()
        for i, r in enumerate(order):
            base = pl.multiple_of(r * width, width)
            there = pl.ds(base, width)
            local[f, there, :] = (x_ref[f, there, :].astype(F32) + conv(w2_ref, base)).astype(BF16)
            if f == 0 and i == 0:
                pl.semaphore_wait(barrier, n - 1)
            for c in range(owners):
                to = r * owners + c

                def send():
                    for k, low, high in pieces(f, c):
                        start = pl.multiple_of(base + (first[c] + low) * UNIT, UNIT)
                        forward(f, k, to, me, start, low, high).start()

                if i < height - 1:
                    send()
                elif counts[c]:
                    pl.when(c != seat)(send)

                    @pl.when(c == seat)
                    def _():
                        size = counts[c] * UNIT
                        recv[me * per + f, pl.ds(0, size), :] = local[
                            f, pl.ds(pl.multiple_of(base + first[c] * UNIT, UNIT), size), :
                        ]

    for copy in loads[4 + per :]:
        copy.wait()

    lane = lax.broadcasted_iota(jnp.int32, (1, channels), 1) // (channels // heads)
    ri = lax.broadcasted_iota(jnp.int32, (block, rows), 0) % SUB
    rj = lax.broadcasted_iota(jnp.int32, (block, rows), 1) % SUB
    same_pixel = ri == rj

    def count_of(device):
        c = lax.rem(device, owners)
        return ((c + 1) * units) // owners - (c * units) // owners

    def unit_rows(device, u, size=1):
        c = lax.rem(device, owners)
        start = (device // owners) * units + (c * units) // owners + u
        return pl.ds(pl.multiple_of(start * UNIT, UNIT), size * UNIT)

    def returning(u, to, source):
        return pltpu.make_async_remote_copy(
            src_ref=fin.at[u, to],
            dst_ref=out_ref.at[:, unit_rows(source, u)],
            send_sem=send2.at[u, to],
            recv_sem=recv2.at[u, source],
            device_id={"frame": to},
            device_id_type=MESH,
        )

    def attend(u):
        x = recv[:, pl.ds(pl.multiple_of(u * UNIT, UNIT), UNIT), :]
        x = x.astype(F32).reshape(frames * UNIT, channels)
        c = x - jnp.mean(x, axis=-1, keepdims=True)
        var = jnp.mean(c * c, axis=-1, keepdims=True)
        normed = (c * lax.rsqrt(var + EPSILON) * pn_ref[...]).astype(BF16)
        for ref, w in ((q_s, wq_ref), (k_s, wk_ref), (v_s, wv_ref)):
            t = dot(normed, w[...]).reshape(frames, UNIT, channels)
            for half in range(halves):
                ref[half] = (
                    t[:, half * SUB : (half + 1) * SUB].reshape(rows, channels).astype(BF16)
                )

        @pl.loop(0, halves)
        def _(half):
            @pl.loop(0, rows // block)
            def _(b):
                qs = pl.ds(pl.multiple_of(b * block, block), block)
                q = q_s[half, qs, :]
                k = k_s[half]
                v = v_s[half]
                total = None
                for h in range(heads):
                    mask = jnp.where(lane == h, 1.0, 0.0).astype(BF16)
                    s = lax.dot_general(
                        q * mask, k, (((1,), (1,)), ((), ())), preferred_element_type=F32
                    )
                    s = s * (sharp_ref[h] * (1.0 / math.sqrt(channels // heads)))
                    s = jnp.where(same_pixel, s, -jnp.inf)
                    e = jnp.exp(s - jnp.max(s, axis=-1, keepdims=True))
                    p = (e * (1.0 / jnp.sum(e, axis=-1, keepdims=True))).astype(BF16)
                    term = dot(p, v * mask)
                    total = term if total is None else total + term
                o_s[half, qs, :] = total

        attended = jnp.concatenate(
            [o_s[half].reshape(frames, SUB, channels) for half in range(halves)], axis=1
        )
        attended = attended.reshape(frames * UNIT, channels).astype(BF16)
        x = recv[:, pl.ds(pl.multiple_of(u * UNIT, UNIT), UNIT), :]
        x = x.astype(F32).reshape(frames * UNIT, channels)
        mixed = (x + dot(attended, wo_ref[...])).astype(BF16)
        edge = jnp.zeros((UNIT, channels), BF16)
        before = jnp.concatenate([edge, mixed[:-UNIT]], axis=0)
        after = jnp.concatenate([mixed[UNIT:], edge], axis=0)
        result = mixed.astype(F32)
        for t, m in enumerate((before, mixed, after)):
            result = result + dot(m, tt_ref[t])
        fin[u] = result.astype(BF16).reshape(n, per, UNIT, channels)
        for i, r in enumerate(order):
            for c in range(owners):

                def send():
                    returning(u, r * owners + c, me).start()

                if i < height - 1:
                    send()
                else:
                    pl.when(c != seat)(send)
        out_ref[:, unit_rows(me, u), :] = fin[u, me]

    cuts = cut(most, parts)
    sizes = sorted(set(counts))
    mine = count_of(me)
    for k in range(parts):
        for size in sizes:
            if cuts[k] >= size:
                continue
            c = counts.index(size)

            @pl.when(mine == size)
            def _():
                for f in range(per):
                    for piece, low, high in pieces(f, c):
                        if piece == k:

                            @pl.loop(1, n)
                            def _(j):
                                to, source = peer(j)
                                forward(f, k, to, source, 0, low, high).wait_recv()

        @pl.loop(cuts[k], cuts[k + 1])
        def _(u):
            @pl.when(u < mine)
            def _():
                attend(u)

    @pl.loop(1, n)
    def _(j):
        to, _ = peer(j)
        for size in sizes:
            c = counts.index(size)

            @pl.when(count_of(to) == size)
            def _():
                for f in range(per):
                    for k, low, high in pieces(f, c):
                        forward(f, k, to, me, 0, low, high).wait_send()

    @pl.loop(0, most)
    def _(u):
        @pl.loop(1, n)
        def _(j):
            to, source = peer(j)

            @pl.when(u < mine)
            def _():
                returning(u, to, me).wait_send()

            @pl.when(u < count_of(source))
            def _():
                returning(u, me, source).wait_recv()


def on_device(n, latent, g1, w1, g2, w2, pn, wq, wk, wv, wo, tt, sharp):
    per, height, width, channels = latent.shape
    pixels = height * width
    frames = n * per
    heads = sharp.shape[0]
    rows = frames * SUB
    halves = UNIT // SUB
    most = max(shares(width, n // height)[1])
    parts = min(2, most)
    hbm = pl.BlockSpec(memory_space=pl.ANY)
    out = pl.pallas_call(
        functools.partial(kernel, n, per, height, width, heads, parts),
        out_shape=pltpu.VMEM((per, pixels, channels), BF16),
        in_specs=[hbm] * 12,
        out_specs=pl.BlockSpec(memory_space=pltpu.VMEM),
        scratch_shapes=[
            pltpu.VMEM((per, pixels, channels), BF16),
            pltpu.VMEM((1, channels), F32),
            pltpu.VMEM((9 * channels, channels), BF16),
            pltpu.VMEM((1, channels), F32),
            pltpu.VMEM((9 * channels, channels), BF16),
            pltpu.VMEM((1, channels), F32),
            pltpu.VMEM(wq.shape, BF16),
            pltpu.VMEM(wk.shape, BF16),
            pltpu.VMEM(wv.shape, BF16),
            pltpu.VMEM(wo.shape, BF16),
            pltpu.VMEM(tt.shape, BF16),
            pltpu.SMEM(sharp.shape, F32),
            pltpu.VMEM(((height + 2) * width, 3 * channels), BF16),
            pltpu.VMEM((pixels, channels), F32),
            pltpu.VMEM((per, pixels, channels), BF16),
            pltpu.VMEM((frames, most * UNIT, channels), BF16),
            pltpu.VMEM((halves, rows, channels), BF16),
            pltpu.VMEM((halves, rows, channels), BF16),
            pltpu.VMEM((halves, rows, channels), BF16),
            pltpu.VMEM((halves, rows, channels), F32),
            pltpu.VMEM((most, n, per, UNIT, channels), BF16),
            pltpu.SemaphoreType.DMA((per + 11,)),
            pltpu.SemaphoreType.DMA((per, parts, n)),
            pltpu.SemaphoreType.DMA((per, parts, n)),
            pltpu.SemaphoreType.DMA((most, n)),
            pltpu.SemaphoreType.DMA((most, n)),
        ],
        compiler_params=pltpu.CompilerParams(
            collective_id=0, has_side_effects=True, vmem_limit_bytes=58 * 1024 * 1024
        ),
        name="block",
    )(
        latent.reshape(per, pixels, channels),
        g1.reshape(1, channels),
        w1.reshape(9 * channels, channels),
        g2.reshape(1, channels),
        w2.reshape(9 * channels, channels),
        pn.reshape(1, channels),
        wq,
        wk,
        wv,
        wo,
        tt,
        sharp,
    )
    return out.reshape(latent.shape)


def solution(mesh):
    split = P(("groups", "frame"), None, None, None)
    return jax.shard_map(
        functools.partial(on_device, mesh.shape["frame"]),
        mesh=mesh,
        in_specs=(split,) + (P(),) * 11,
        out_specs=split,
        check_vma=False,
    )
```

```python
import functools
import math

import jax
import jax.numpy as jnp
from jax import lax
from jax.experimental import pallas as pl
from jax.experimental.pallas import tpu as pltpu
from jax.sharding import PartitionSpec as P

GROUPS = 32
EPSILON = 1e-05
SUB = 8
UNIT = 16
F32 = jnp.float32
BF16 = jnp.bfloat16
MESH = pl.DeviceIdType.MESH


def dot(a, b):
    return jnp.dot(a, b, preferred_element_type=F32)


def shares(width, owners):
    units = width // UNIT
    first = [c * units // owners for c in range(owners + 1)]
    return first, [first[c + 1] - first[c] for c in range(owners)]


def cut(most, parts):
    return [most * k // parts for k in range(parts + 1)]


def kernel(
    n,
    per,
    height,
    width,
    heads,
    parts,
    batches,
    x_hbm,
    g1_hbm,
    w1_hbm,
    g2_hbm,
    w2_hbm,
    pn_hbm,
    wq_hbm,
    wk_hbm,
    wv_hbm,
    wo_hbm,
    tt_hbm,
    sharp_hbm,
    out_ref,
    x_ref,
    g1_ref,
    w1_ref,
    g2_ref,
    w2_ref,
    pn_ref,
    wq_ref,
    wk_ref,
    wv_ref,
    wo_ref,
    tt_ref,
    sharp_ref,
    act,
    hid,
    local,
    recv,
    q_s,
    k_s,
    v_s,
    o_s,
    fin,
    load,
    send1,
    recv1,
    send2,
    recv2,
):
    me = lax.axis_index("frame")
    pixels = height * width
    channels = x_ref.shape[-1]
    frames = n * per
    owners = n // height
    units = width // UNIT
    first, counts = shares(width, owners)
    most = max(counts)
    rows = frames * SUB
    block = min(rows, 256)
    halves = UNIT // SUB
    plane = me // owners
    seat = me % owners
    order = [
        height - 1 - plane,
        lax.rem(plane + height // 2, height),
        plane + 1 - 2 * lax.rem(plane, 2),
        plane,
    ]

    def pieces(f, c):
        cuts = cut(most, parts) if f == per - 1 else [0, most]
        return [
            (k, cuts[k], min(cuts[k + 1], counts[c]))
            for k in range(len(cuts) - 1)
            if cuts[k] < counts[c]
        ]

    def peer(j):
        return lax.rem(me + j, n), lax.rem(me + n - j, n)

    loads = []
    for source, target in (
        (x_hbm.at[0], x_ref.at[0]),
        (g1_hbm, g1_ref),
        (w1_hbm, w1_ref),
        (g2_hbm, g2_ref),
        (w2_hbm, w2_ref),
        *((x_hbm.at[f], x_ref.at[f]) for f in range(1, per)),
        (pn_hbm, pn_ref),
        (wq_hbm, wq_ref),
        (wk_hbm, wk_ref),
        (wv_hbm, wv_ref),
        (wo_hbm, wo_ref),
        (tt_hbm, tt_ref),
        (sharp_hbm, sharp_ref),
    ):
        loads.append(pltpu.make_async_copy(source, target, load.at[len(loads)]))
    for copy in loads:
        copy.start()

    barrier = pltpu.get_barrier_semaphore()

    @pl.loop(1, n)
    def _(j):
        to, _ = peer(lax.rem(j + n // 2 - 1, n - 1) + 1)
        pl.semaphore_signal(barrier, inc=1, device_id={"frame": to}, device_id_type=MESH)

    act[pl.ds(0, width), :] = jnp.zeros((width, 3 * channels), BF16)
    act[pl.ds((height + 1) * width, width), :] = jnp.zeros((width, 3 * channels), BF16)

    per_group = channels // GROUPS
    lanes = lax.broadcasted_iota(jnp.int32, (8, channels), 1)
    column = lax.broadcasted_iota(jnp.int32, (width, channels), 0)

    def group_mean(values):
        total = jnp.broadcast_to(values, (8, channels))
        step = 1
        while step < per_group:
            total = total + jnp.where(
                (lanes // step) % 2 == 0,
                pltpu.roll(total, channels - step, 1),
                pltpu.roll(total, step, 1),
            )
            step *= 2
        return total[:1] * (1.0 / per_group)

    def fold(v):
        return jnp.sum(v.reshape(width // 8, 8, channels), axis=0)

    def moments(shift, s1, s2):
        m1 = jnp.sum(s1, axis=0, keepdims=True) * (1.0 / pixels)
        m2 = jnp.sum(s2, axis=0, keepdims=True) * (1.0 / pixels)
        own = shift + m1
        mean = group_mean(own)
        off = own - mean
        var = group_mean(jnp.maximum(m2 - m1 * m1, 0.0) + off * off)
        return mean, lax.rsqrt(var + EPSILON)

    def row_of(i):
        return pl.ds(i * width, width)

    def activate(value, mean, inv, gain):
        half = inv * gain * 0.5
        for i in range(height):
            v = (value(i) - mean) * half
            y = (v * jnp.tanh(v) + v).astype(BF16)
            wide = y.astype(F32)
            there = row_of(i + 1)
            act[there, pl.ds(0, channels)] = jnp.where(
                column == 0, 0.0, pltpu.roll(wide, 1, 0)
            ).astype(BF16)
            act[there, pl.ds(channels, channels)] = y
            act[there, pl.ds(2 * channels, channels)] = jnp.where(
                column == width - 1, 0.0, pltpu.roll(wide, width - 1, 0)
            ).astype(BF16)

    def conv(w_ref, start):
        total = None
        for a in range(3):
            term = dot(
                act[pl.ds(start + a * width, width), :],
                w_ref[pl.ds(a * 3 * channels, 3 * channels), :],
            )
            total = term if total is None else total + term
        return total

    def sums(value, shift, s1, s2):
        d = value - shift
        return s1 + fold(d), s2 + fold(d * d)

    def forward(f, k, to, source, start, low, high):
        return pltpu.make_async_remote_copy(
            src_ref=local.at[f, pl.ds(start, (high - low) * UNIT)],
            dst_ref=recv.at[source * per + f, pl.ds(low * UNIT, (high - low) * UNIT)],
            send_sem=send1.at[f],
            recv_sem=recv1.at[f + k],
            device_id={"frame": to},
            device_id_type=MESH,
        )

    def everything(ref, sem):
        pltpu.make_async_copy(ref, ref, sem).wait()

    def ship(f, part, r, c):
        for k, low, high in pieces(f, c):
            if k == part:
                start = pl.multiple_of(r * width + (first[c] + low) * UNIT, UNIT)
                forward(f, k, r * owners + c, me, start, low, high).start()

    zero = jnp.zeros((8, channels), F32)

    for f in range(per):
        if f == 0:
            loads[0].wait()
            loads[1].wait()
        else:
            loads[4 + f].wait()

        def pixels_of(i):
            return x_ref[f, row_of(i), :].astype(F32)

        shift = pixels_of(0)[:1]
        s1, s2 = zero, zero
        for i in range(height):
            s1, s2 = sums(pixels_of(i), shift, s1, s2)
        activate(pixels_of, *moments(shift, s1, s2), g1_ref[...])

        if f == 0:
            loads[2].wait()
        shift, s1, s2 = None, zero, zero
        for i in range(height):
            value = conv(w1_ref, i * width)
            hid[row_of(i), :] = value
            if shift is None:
                shift = value[:1]
            s1, s2 = sums(value, shift, s1, s2)
        if f == 0:
            loads[3].wait()
        activate(lambda i: hid[row_of(i), :], *moments(shift, s1, s2), g2_ref[...])

        if f == 0:
            loads[4].wait()
        for i, r in enumerate(order):
            base = pl.multiple_of(r * width, width)
            there = pl.ds(base, width)
            local[f, there, :] = (x_ref[f, there, :].astype(F32) + conv(w2_ref, base)).astype(BF16)
            if f == 0 and i == 0:
                pl.semaphore_wait(barrier, n - 1)
            for c in range(owners):
                if i < height - 1:
                    ship(f, 0, r, c)
                elif counts[c]:
                    pl.when(c != seat)(functools.partial(ship, f, 0, r, c))

                    @pl.when(c == seat)
                    def _():
                        size = counts[c] * UNIT
                        recv[me * per + f, pl.ds(0, size), :] = local[
                            f, pl.ds(pl.multiple_of(base + first[c] * UNIT, UNIT), size), :
                        ]

        for k in range(1, parts if f == per - 1 else 1):
            for i, r in enumerate(order):
                for c in range(owners):
                    if i < height - 1:
                        ship(f, k, r, c)
                    else:
                        pl.when(c != seat)(functools.partial(ship, f, k, r, c))

    for copy in loads[4 + per :]:
        copy.wait()

    lane = lax.broadcasted_iota(jnp.int32, (1, channels), 1) // (channels // heads)
    ri = lax.broadcasted_iota(jnp.int32, (block, rows), 0) % SUB
    rj = lax.broadcasted_iota(jnp.int32, (block, rows), 1) % SUB
    same_pixel = ri == rj

    def count_of(device):
        c = lax.rem(device, owners)
        return ((c + 1) * units) // owners - (c * units) // owners

    def unit_rows(device, u, size=1):
        c = lax.rem(device, owners)
        start = (device // owners) * units + (c * units) // owners + u
        return pl.ds(pl.multiple_of(start * UNIT, UNIT), size * UNIT)

    def returning(q, size, to, source):
        return pltpu.make_async_remote_copy(
            src_ref=fin.at[q, to, :, pl.ds(0, size * UNIT)],
            dst_ref=out_ref.at[:, unit_rows(source, batches[q][0], size)],
            send_sem=send2.at[q],
            recv_sem=recv2,
            device_id={"frame": to},
            device_id_type=MESH,
        )

    def attend(q, u):
        x = recv[:, pl.ds(pl.multiple_of(u * UNIT, UNIT), UNIT), :]
        x = x.astype(F32).reshape(frames * UNIT, channels)
        c = x - jnp.mean(x, axis=-1, keepdims=True)
        var = jnp.mean(c * c, axis=-1, keepdims=True)
        normed = (c * lax.rsqrt(var + EPSILON) * pn_ref[...]).astype(BF16)
        for ref, w in ((q_s, wq_ref), (k_s, wk_ref), (v_s, wv_ref)):
            t = dot(normed, w[...]).reshape(frames, UNIT, channels)
            for half in range(halves):
                ref[half] = (
                    t[:, half * SUB : (half + 1) * SUB].reshape(rows, channels).astype(BF16)
                )

        @pl.loop(0, halves)
        def _(half):
            @pl.loop(0, rows // block)
            def _(b):
                qs = pl.ds(pl.multiple_of(b * block, block), block)
                q = q_s[half, qs, :]
                k = k_s[half]
                v = v_s[half]
                total = None
                for h in range(heads):
                    mask = jnp.where(lane == h, 1.0, 0.0).astype(BF16)
                    s = lax.dot_general(
                        q * mask, k, (((1,), (1,)), ((), ())), preferred_element_type=F32
                    )
                    s = s * (sharp_ref[h] * (1.0 / math.sqrt(channels // heads)))
                    s = jnp.where(same_pixel, s, -jnp.inf)
                    e = jnp.exp(s - jnp.max(s, axis=-1, keepdims=True))
                    p = (e * (1.0 / jnp.sum(e, axis=-1, keepdims=True))).astype(BF16)
                    term = dot(p, v * mask)
                    total = term if total is None else total + term
                o_s[half, qs, :] = total

        attended = jnp.concatenate(
            [o_s[half].reshape(frames, SUB, channels) for half in range(halves)], axis=1
        )
        attended = attended.reshape(frames * UNIT, channels).astype(BF16)
        x = recv[:, pl.ds(pl.multiple_of(u * UNIT, UNIT), UNIT), :]
        x = x.astype(F32).reshape(frames * UNIT, channels)
        mixed = (x + dot(attended, wo_ref[...])).astype(BF16)
        edge = jnp.zeros((UNIT, channels), BF16)
        before = jnp.concatenate([edge, mixed[:-UNIT]], axis=0)
        after = jnp.concatenate([mixed[UNIT:], edge], axis=0)
        result = mixed.astype(F32)
        for t, m in enumerate((before, mixed, after)):
            result = result + dot(m, tt_ref[t])
        place = pl.ds(pl.multiple_of((u - batches[q][0]) * UNIT, UNIT), UNIT)
        fin[q, :, :, place, :] = result.astype(BF16).reshape(n, per, UNIT, channels)

    def give(q, size):
        for i, r in enumerate(order):
            for c in range(owners):

                def send():
                    returning(q, size, r * owners + c, me).start()

                if i < height - 1:
                    send()
                else:
                    pl.when(c != seat)(send)
        out_ref[:, unit_rows(me, batches[q][0], size), :] = fin[q, me, :, pl.ds(0, size * UNIT), :]

    cuts = cut(most, parts)
    sizes = sorted(set(counts))
    mine = count_of(me)
    for k in range(parts):
        for size in sizes:
            if cuts[k] >= size:
                continue
            c = counts.index(size)

            @pl.when(mine == size)
            def _():
                for f in range(per):
                    for piece, low, high in pieces(f, c):
                        if piece == k:
                            arrived = recv.at[pl.ds(0, n - 1), pl.ds(0, (high - low) * UNIT)]
                            everything(arrived, recv1.at[f + k])

        for q, (low, high) in enumerate(batches):
            if not cuts[k] <= low < cuts[k + 1]:
                continue

            @pl.loop(low, high)
            def _(u):
                @pl.when(u < mine)
                def _():
                    attend(q, u)

            for size in sizes:
                if low < size:
                    pl.when(mine == size)(functools.partial(give, q, min(high, size) - low))

    for size in sizes:

        @pl.when(mine == size)
        def _():
            others = pl.ds(0, pixels - size * UNIT)
            for f in range(per):
                everything(local.at[f, others], send1.at[f])
            for q, (low, high) in enumerate(batches):
                if low < size:
                    sent = pl.ds(0, (min(high, size) - low) * UNIT)
                    everything(fin.at[q, pl.ds(0, n - 1), :, sent], send2.at[q])
            everything(out_ref.at[:, others], recv2)


def on_device(n, latent, g1, w1, g2, w2, pn, wq, wk, wv, wo, tt, sharp):
    per, height, width, channels = latent.shape
    pixels = height * width
    frames = n * per
    heads = sharp.shape[0]
    rows = frames * SUB
    halves = UNIT // SUB
    most = max(shares(width, n // height)[1])
    parts = min(4, most)
    batches = [
        (low, min(low + 1, high))
        for cuts in [cut(most, parts)]
        for start, high in zip(cuts[:-1], cuts[1:])
        for low in range(start, high, 1)
    ]
    hbm = pl.BlockSpec(memory_space=pl.ANY)
    out = pl.pallas_call(
        functools.partial(kernel, n, per, height, width, heads, parts, batches),
        out_shape=pltpu.VMEM((per, pixels, channels), BF16),
        in_specs=[hbm] * 12,
        out_specs=pl.BlockSpec(memory_space=pltpu.VMEM),
        scratch_shapes=[
            pltpu.VMEM((per, pixels, channels), BF16),
            pltpu.VMEM((1, channels), F32),
            pltpu.VMEM((9 * channels, channels), BF16),
            pltpu.VMEM((1, channels), F32),
            pltpu.VMEM((9 * channels, channels), BF16),
            pltpu.VMEM((1, channels), F32),
            pltpu.VMEM(wq.shape, BF16),
            pltpu.VMEM(wk.shape, BF16),
            pltpu.VMEM(wv.shape, BF16),
            pltpu.VMEM(wo.shape, BF16),
            pltpu.VMEM(tt.shape, BF16),
            pltpu.SMEM(sharp.shape, F32),
            pltpu.VMEM(((height + 2) * width, 3 * channels), BF16),
            pltpu.VMEM((pixels, channels), F32),
            pltpu.VMEM((per, pixels, channels), BF16),
            pltpu.VMEM((frames, most * UNIT, channels), BF16),
            pltpu.VMEM((halves, rows, channels), BF16),
            pltpu.VMEM((halves, rows, channels), BF16),
            pltpu.VMEM((halves, rows, channels), BF16),
            pltpu.VMEM((halves, rows, channels), F32),
            pltpu.VMEM((len(batches), n, per, 1 * UNIT, channels), BF16),
            pltpu.SemaphoreType.DMA((per + 11,)),
            pltpu.SemaphoreType.DMA((per,)),
            pltpu.SemaphoreType.DMA((per + parts - 1,)),
            pltpu.SemaphoreType.DMA((len(batches),)),
            pltpu.SemaphoreType.DMA,
        ],
        compiler_params=pltpu.CompilerParams(
            collective_id=0, has_side_effects=True, vmem_limit_bytes=58 * 1024 * 1024
        ),
        name="block",
    )(
        latent.reshape(per, pixels, channels),
        g1.reshape(1, channels),
        w1.reshape(9 * channels, channels),
        g2.reshape(1, channels),
        w2.reshape(9 * channels, channels),
        pn.reshape(1, channels),
        wq,
        wk,
        wv,
        wo,
        tt,
        sharp,
    )
    return out.reshape(latent.shape)


def solution(mesh):
    split = P(("groups", "frame"), None, None, None)
    return jax.shard_map(
        functools.partial(on_device, mesh.shape["frame"]),
        mesh=mesh,
        in_specs=(split,) + (P(),) * 11,
        out_specs=split,
        check_vma=False,
    )
```

```python
import functools
import math

import jax
import jax.numpy as jnp
from jax import lax
from jax.experimental import pallas as pl
from jax.experimental.pallas import tpu as pltpu
from jax.sharding import PartitionSpec as P

GROUPS = 32
EPSILON = 1e-05
SUB = 8
UNIT = 16
F32 = jnp.float32
BF16 = jnp.bfloat16
MESH = pl.DeviceIdType.MESH


def dot(a, b):
    return jnp.dot(a, b, preferred_element_type=F32)


def shares(width, owners):
    units = width // UNIT
    first = [c * units // owners for c in range(owners + 1)]
    return first, [first[c + 1] - first[c] for c in range(owners)]


def cut(most):
    return [*range(max(most - 1, 1)), most]


def kernel(
    n,
    per,
    height,
    width,
    heads,
    batches,
    x_hbm,
    g1_hbm,
    w1_hbm,
    g2_hbm,
    w2_hbm,
    pn_hbm,
    wq_hbm,
    wk_hbm,
    wv_hbm,
    wo_hbm,
    tt_hbm,
    sharp_hbm,
    out_ref,
    x_ref,
    g1_ref,
    w1_ref,
    g2_ref,
    w2_ref,
    pn_ref,
    wq_ref,
    wk_ref,
    wv_ref,
    wo_ref,
    tt_ref,
    sharp_ref,
    act,
    hid,
    local,
    recv,
    q_s,
    k_s,
    v_s,
    o_s,
    fin,
    load,
    send1,
    recv1,
    send2,
    recv2,
):
    me = lax.axis_index("frame")
    pixels = height * width
    channels = x_ref.shape[-1]
    frames = n * per
    owners = n // height
    units = width // UNIT
    first, counts = shares(width, owners)
    most = max(counts)
    parts = len(batches)
    rows = frames * SUB
    block = min(rows, 256)
    halves = UNIT // SUB
    plane = me // owners
    seat = me % owners
    order = [
        height - 1 - plane,
        lax.rem(plane + height // 2, height),
        plane + 1 - 2 * lax.rem(plane, 2),
        plane,
    ]

    def pieces(f, c):
        cuts = cut(most) if f == per - 1 else [0, most]
        return [
            (k, cuts[k], min(cuts[k + 1], counts[c]))
            for k in range(len(cuts) - 1)
            if cuts[k] < counts[c]
        ]

    def peer(j):
        return lax.rem(me + j, n), lax.rem(me + n - j, n)

    loads = []
    for source, target in (
        (x_hbm.at[0], x_ref.at[0]),
        (g1_hbm, g1_ref),
        (w1_hbm, w1_ref),
        (g2_hbm, g2_ref),
        (w2_hbm, w2_ref),
        *((x_hbm.at[f], x_ref.at[f]) for f in range(1, per)),
        (pn_hbm, pn_ref),
        (wq_hbm, wq_ref),
        (wk_hbm, wk_ref),
        (wv_hbm, wv_ref),
        (wo_hbm, wo_ref),
        (tt_hbm, tt_ref),
        (sharp_hbm, sharp_ref),
    ):
        loads.append(pltpu.make_async_copy(source, target, load.at[len(loads)]))
    for copy in loads:
        copy.start()

    barrier = pltpu.get_barrier_semaphore()

    @pl.loop(1, n)
    def _(j):
        to, _ = peer(lax.rem(j + n // 2 - 1, n - 1) + 1)
        pl.semaphore_signal(barrier, inc=1, device_id={"frame": to}, device_id_type=MESH)

    act[pl.ds(0, width), :] = jnp.zeros((width, 3 * channels), BF16)
    act[pl.ds((height + 1) * width, width), :] = jnp.zeros((width, 3 * channels), BF16)

    per_group = channels // GROUPS
    lanes = lax.broadcasted_iota(jnp.int32, (8, channels), 1)
    column = lax.broadcasted_iota(jnp.int32, (width, channels), 0)

    def group_mean(values):
        total = jnp.broadcast_to(values, (8, channels))
        step = 1
        while step < per_group:
            total = total + jnp.where(
                (lanes // step) % 2 == 0,
                pltpu.roll(total, channels - step, 1),
                pltpu.roll(total, step, 1),
            )
            step *= 2
        return total[:1] * (1.0 / per_group)

    def fold(v):
        return jnp.sum(v.reshape(width // 8, 8, channels), axis=0)

    def moments(shift, s1, s2):
        m1 = group_mean(jnp.sum(s1, axis=0, keepdims=True) * (1.0 / pixels))
        m2 = group_mean(jnp.sum(s2, axis=0, keepdims=True) * (1.0 / pixels))
        return shift + m1, lax.rsqrt(jnp.maximum(m2 - m1 * m1, 0.0) + EPSILON)

    def row_of(i):
        return pl.ds(i * width if isinstance(i, int) else pl.multiple_of(i * width, width), width)

    def activate(value, mean, inv, gain):
        half = inv * gain * 0.5
        @pl.loop(0, height)
        def _(i):
            v = (value(i) - mean) * half
            y = (v * jnp.tanh(v) + v).astype(BF16)
            wide = y.astype(F32)
            there = pl.ds(pl.multiple_of((i + 1) * width, width), width)
            act[there, pl.ds(0, channels)] = jnp.where(
                column == 0, 0.0, pltpu.roll(wide, 1, 0)
            ).astype(BF16)
            act[there, pl.ds(channels, channels)] = y
            act[there, pl.ds(2 * channels, channels)] = jnp.where(
                column == width - 1, 0.0, pltpu.roll(wide, width - 1, 0)
            ).astype(BF16)

    def conv(w_ref, start):
        total = None
        for a in range(3):
            term = dot(
                act[pl.ds(start + a * width, width), :],
                w_ref[pl.ds(a * 3 * channels, 3 * channels), :],
            )
            total = term if total is None else total + term
        return total

    def sums(value, shift, s1, s2):
        d = value - shift
        return s1 + fold(d), s2 + fold(d * d)

    def forward(f, k, to, source, start, low, high):
        return pltpu.make_async_remote_copy(
            src_ref=local.at[f, pl.ds(start, (high - low) * UNIT)],
            dst_ref=recv.at[source * per + f, pl.ds(low * UNIT, (high - low) * UNIT)],
            send_sem=send1.at[f],
            recv_sem=recv1.at[f + k],
            device_id={"frame": to},
            device_id_type=MESH,
        )

    def everything(ref, sem):
        pltpu.make_async_copy(ref, ref, sem).wait()

    def ship(f, part, r, c):
        for k, low, high in pieces(f, c):
            if k == part:
                start = pl.multiple_of(r * width + (first[c] + low) * UNIT, UNIT)
                forward(f, k, r * owners + c, me, start, low, high).start()

    zero = jnp.zeros((8, channels), F32)

    for f in range(per):
        if f == 0:
            loads[0].wait()
            loads[1].wait()
        else:
            loads[4 + f].wait()

        def pixels_of(i):
            return x_ref[f, row_of(i), :].astype(F32)

        shift = group_mean(pixels_of(0)[:1])
        s1, s2 = zero, zero
        for i in range(height):
            s1, s2 = sums(pixels_of(i), shift, s1, s2)
        activate(pixels_of, *moments(shift, s1, s2), g1_ref[...])

        if f == 0:
            loads[2].wait()
        shift, s1, s2 = None, zero, zero
        for i in range(height):
            value = conv(w1_ref, i * width)
            hid[row_of(i), :] = value
            if shift is None:
                shift = group_mean(value[:1])
            s1, s2 = sums(value, shift, s1, s2)
        if f == 0:
            loads[3].wait()
        activate(lambda i: hid[row_of(i), :], *moments(shift, s1, s2), g2_ref[...])

        if f == 0:
            loads[4].wait()
        for i, r in enumerate(order):
            base = pl.multiple_of(r * width, width)
            there = pl.ds(base, width)
            local[f, there, :] = (x_ref[f, there, :].astype(F32) + conv(w2_ref, base)).astype(BF16)
            if f == 0 and i == 0:
                pl.semaphore_wait(barrier, n - 1)
            for c in range(owners):
                if i < height - 1:
                    ship(f, 0, r, c)
                elif counts[c]:
                    pl.when(c != seat)(functools.partial(ship, f, 0, r, c))

                    @pl.when(c == seat)
                    def _():
                        size = counts[c] * UNIT
                        recv[me * per + f, pl.ds(0, size), :] = local[
                            f, pl.ds(pl.multiple_of(base + first[c] * UNIT, UNIT), size), :
                        ]

        for k in range(1, parts if f == per - 1 else 1):
            for i, r in enumerate(order):
                for c in range(owners):
                    if i < height - 1:
                        ship(f, k, r, c)
                    else:
                        pl.when(c != seat)(functools.partial(ship, f, k, r, c))

    for copy in loads[4 + per :]:
        copy.wait()

    lane = lax.broadcasted_iota(jnp.int32, (1, channels), 1) // (channels // heads)
    ri = lax.broadcasted_iota(jnp.int32, (block, rows), 0) % SUB
    rj = lax.broadcasted_iota(jnp.int32, (block, rows), 1) % SUB
    same_pixel = ri == rj

    def count_of(device):
        c = lax.rem(device, owners)
        return ((c + 1) * units) // owners - (c * units) // owners

    def unit_rows(device, u, size=1):
        c = lax.rem(device, owners)
        start = (device // owners) * units + (c * units) // owners + u
        return pl.ds(pl.multiple_of(start * UNIT, UNIT), size * UNIT)

    def returning(q, size, to, source):
        return pltpu.make_async_remote_copy(
            src_ref=fin.at[q, to, :, pl.ds(0, size * UNIT)],
            dst_ref=out_ref.at[:, unit_rows(source, batches[q][0], size)],
            send_sem=send2.at[q],
            recv_sem=recv2,
            device_id={"frame": to},
            device_id_type=MESH,
        )

    def attend(q, u):
        x = recv[:, pl.ds(pl.multiple_of(u * UNIT, UNIT), UNIT), :]
        x = x.astype(F32).reshape(frames * UNIT, channels)
        c = x - jnp.mean(x, axis=-1, keepdims=True)
        var = jnp.mean(c * c, axis=-1, keepdims=True)
        normed = (c * lax.rsqrt(var + EPSILON) * pn_ref[...]).astype(BF16)
        for ref, w in ((q_s, wq_ref), (k_s, wk_ref), (v_s, wv_ref)):
            t = dot(normed, w[...]).reshape(frames, UNIT, channels)
            for half in range(halves):
                ref[half] = (
                    t[:, half * SUB : (half + 1) * SUB].reshape(rows, channels).astype(BF16)
                )

        @pl.loop(0, halves)
        def _(half):
            @pl.loop(0, rows // block)
            def _(b):
                qs = pl.ds(pl.multiple_of(b * block, block), block)
                q = q_s[half, qs, :]
                k = k_s[half]
                v = v_s[half]
                total = None
                for h in range(heads):
                    mask = jnp.where(lane == h, 1.0, 0.0).astype(BF16)
                    s = lax.dot_general(
                        q * mask, k, (((1,), (1,)), ((), ())), preferred_element_type=F32
                    )
                    s = s * (sharp_ref[h] * (1.0 / math.sqrt(channels // heads)))
                    s = jnp.where(same_pixel, s, -jnp.inf)
                    e = jnp.exp(s - jnp.max(s, axis=-1, keepdims=True))
                    p = (e * (1.0 / jnp.sum(e, axis=-1, keepdims=True))).astype(BF16)
                    term = dot(p, v * mask)
                    total = term if total is None else total + term
                o_s[half, qs, :] = total

        attended = jnp.concatenate(
            [o_s[half].reshape(frames, SUB, channels) for half in range(halves)], axis=1
        )
        attended = attended.reshape(frames * UNIT, channels).astype(BF16)
        x = recv[:, pl.ds(pl.multiple_of(u * UNIT, UNIT), UNIT), :]
        x = x.astype(F32).reshape(frames * UNIT, channels)
        mixed = (x + dot(attended, wo_ref[...])).astype(BF16)
        edge = jnp.zeros((UNIT, channels), BF16)
        before = jnp.concatenate([edge, mixed[:-UNIT]], axis=0)
        after = jnp.concatenate([mixed[UNIT:], edge], axis=0)
        result = mixed.astype(F32)
        for t, m in enumerate((before, mixed, after)):
            result = result + dot(m, tt_ref[t])
        place = pl.ds(pl.multiple_of((u - batches[q][0]) * UNIT, UNIT), UNIT)
        fin[q, :, :, place, :] = result.astype(BF16).reshape(n, per, UNIT, channels)

    def give(q, size):
        for i, r in enumerate(order):
            for c in range(owners):

                def send():
                    returning(q, size, r * owners + c, me).start()

                if i < height - 1:
                    send()
                else:
                    pl.when(c != seat)(send)
        out_ref[:, unit_rows(me, batches[q][0], size), :] = fin[q, me, :, pl.ds(0, size * UNIT), :]

    cuts = cut(most)
    sizes = sorted(set(counts))
    mine = count_of(me)
    for k in range(parts):
        for size in sizes:
            if cuts[k] >= size:
                continue
            c = counts.index(size)

            @pl.when(mine == size)
            def _():
                for f in range(per):
                    for piece, low, high in pieces(f, c):
                        if piece == k:
                            arrived = recv.at[pl.ds(0, n - 1), pl.ds(0, (high - low) * UNIT)]
                            everything(arrived, recv1.at[f + k])

        for q, (low, high) in enumerate(batches):
            if not cuts[k] <= low < cuts[k + 1]:
                continue

            @pl.loop(low, high)
            def _(u):
                @pl.when(u < mine)
                def _():
                    attend(q, u)

            for size in sizes:
                if low < size:
                    pl.when(mine == size)(functools.partial(give, q, min(high, size) - low))

    for size in sizes:

        @pl.when(mine == size)
        def _():
            others = pl.ds(0, pixels - size * UNIT)
            for f in range(per):
                everything(local.at[f, others], send1.at[f])
            for q, (low, high) in enumerate(batches):
                if low < size:
                    sent = pl.ds(0, (min(high, size) - low) * UNIT)
                    everything(fin.at[q, pl.ds(0, n - 1), :, sent], send2.at[q])
            everything(out_ref.at[:, others], recv2)


def on_device(n, latent, g1, w1, g2, w2, pn, wq, wk, wv, wo, tt, sharp):
    per, height, width, channels = latent.shape
    pixels = height * width
    frames = n * per
    heads = sharp.shape[0]
    rows = frames * SUB
    halves = UNIT // SUB
    most = max(shares(width, n // height)[1])
    cuts = cut(most)
    batches = list(zip(cuts[:-1], cuts[1:]))
    hbm = pl.BlockSpec(memory_space=pl.ANY)
    out = pl.pallas_call(
        functools.partial(kernel, n, per, height, width, heads, batches),
        out_shape=pltpu.VMEM((per, pixels, channels), BF16),
        in_specs=[hbm] * 12,
        out_specs=pl.BlockSpec(memory_space=pltpu.VMEM),
        scratch_shapes=[
            pltpu.VMEM((per, pixels, channels), BF16),
            pltpu.VMEM((1, channels), F32),
            pltpu.VMEM((9 * channels, channels), BF16),
            pltpu.VMEM((1, channels), F32),
            pltpu.VMEM((9 * channels, channels), BF16),
            pltpu.VMEM((1, channels), F32),
            pltpu.VMEM(wq.shape, BF16),
            pltpu.VMEM(wk.shape, BF16),
            pltpu.VMEM(wv.shape, BF16),
            pltpu.VMEM(wo.shape, BF16),
            pltpu.VMEM(tt.shape, BF16),
            pltpu.SMEM(sharp.shape, F32),
            pltpu.VMEM(((height + 2) * width, 3 * channels), BF16),
            pltpu.VMEM((pixels, channels), F32),
            pltpu.VMEM((per, pixels, channels), BF16),
            pltpu.VMEM((frames, most * UNIT, channels), BF16),
            pltpu.VMEM((halves, rows, channels), BF16),
            pltpu.VMEM((halves, rows, channels), BF16),
            pltpu.VMEM((halves, rows, channels), BF16),
            pltpu.VMEM((halves, rows, channels), F32),
            pltpu.VMEM((len(batches), n, per, max(b - a for a, b in batches) * UNIT, channels), BF16),
            pltpu.SemaphoreType.DMA((per + 11,)),
            pltpu.SemaphoreType.DMA((per,)),
            pltpu.SemaphoreType.DMA((per + len(batches) - 1,)),
            pltpu.SemaphoreType.DMA((len(batches),)),
            pltpu.SemaphoreType.DMA,
        ],
        compiler_params=pltpu.CompilerParams(
            collective_id=0, has_side_effects=True, vmem_limit_bytes=58 * 1024 * 1024
        ),
        name="block",
    )(
        latent.reshape(per, pixels, channels),
        g1.reshape(1, channels),
        w1.reshape(9 * channels, channels),
        g2.reshape(1, channels),
        w2.reshape(9 * channels, channels),
        pn.reshape(1, channels),
        wq,
        wk,
        wv,
        wo,
        tt,
        sharp,
    )
    return out.reshape(latent.shape)


def solution(mesh):
    split = P(("groups", "frame"), None, None, None)
    return jax.shard_map(
        functools.partial(on_device, mesh.shape["frame"]),
        mesh=mesh,
        in_specs=(split,) + (P(),) * 11,
        out_specs=split,
        check_vma=False,
    )
```

```python
import functools
import math

import jax
import jax.numpy as jnp
from jax import lax
from jax.experimental import pallas as pl
from jax.experimental.pallas import tpu as pltpu
from jax.sharding import PartitionSpec as P

GROUPS = 32
EPSILON = 1e-05
SUB = 8
UNIT = 16
F32 = jnp.float32
BF16 = jnp.bfloat16
MESH = pl.DeviceIdType.MESH


def dot(a, b):
    return jnp.dot(a, b, preferred_element_type=F32)


def shares(width, owners):
    units = width // UNIT
    first = [c * units // owners for c in range(owners + 1)]
    return first, [first[c + 1] - first[c] for c in range(owners)]


def cut(most):
    return [*range(max(most - 1, 1)), most]


def kernel(
    n,
    per,
    height,
    width,
    heads,
    batches,
    x_hbm,
    g1_hbm,
    w1_hbm,
    g2_hbm,
    w2_hbm,
    pn_hbm,
    wq_hbm,
    wk_hbm,
    wv_hbm,
    wo_hbm,
    tt_hbm,
    sharp_hbm,
    out_ref,
    x_ref,
    g1_ref,
    w1_ref,
    g2_ref,
    w2_ref,
    pn_ref,
    wq_ref,
    wk_ref,
    wv_ref,
    wo_ref,
    tt_ref,
    sharp_ref,
    act,
    hid,
    local,
    recv,
    q_s,
    k_s,
    v_s,
    o_s,
    fin,
    load,
    send1,
    recv1,
    send2,
    recv2,
):
    me = lax.axis_index("frame")
    pixels = height * width
    channels = x_ref.shape[-1]
    frames = n * per
    owners = n // height
    units = width // UNIT
    first, counts = shares(width, owners)
    most = max(counts)
    parts = len(batches)
    rows = frames * SUB
    block = min(rows, 256)
    halves = UNIT // SUB
    plane = me // owners
    seat = me % owners

    def owner(r, c):
        return r * owners + lax.rem(c + owners // 2 * lax.rem(r, 2), owners)

    def share_of(device):
        return lax.rem(device + owners - owners // 2 * lax.rem(device // owners, 2), owners)

    own_share = share_of(me)
    order = [
        height - 1 - plane,
        lax.rem(plane + height // 2, height),
        plane + 1 - 2 * lax.rem(plane, 2),
        plane,
    ]

    def pieces(f, c):
        cuts = cut(most) if f == per - 1 else [0, most]
        return [
            (k, cuts[k], min(cuts[k + 1], counts[c]))
            for k in range(len(cuts) - 1)
            if cuts[k] < counts[c]
        ]

    def peer(j):
        return lax.rem(me + j, n), lax.rem(me + n - j, n)

    loads = []
    for source, target in (
        (x_hbm.at[0], x_ref.at[0]),
        (g1_hbm, g1_ref),
        (w1_hbm, w1_ref),
        (g2_hbm, g2_ref),
        (w2_hbm, w2_ref),
        *((x_hbm.at[f], x_ref.at[f]) for f in range(1, per)),
        (pn_hbm, pn_ref),
        (wq_hbm, wq_ref),
        (wk_hbm, wk_ref),
        (wv_hbm, wv_ref),
        (wo_hbm, wo_ref),
        (tt_hbm, tt_ref),
        (sharp_hbm, sharp_ref),
    ):
        loads.append(pltpu.make_async_copy(source, target, load.at[len(loads)]))
    for copy in loads:
        copy.start()

    barrier = pltpu.get_barrier_semaphore()

    @pl.loop(1, n)
    def _(j):
        to, _ = peer(lax.rem(j + n // 2 - 1, n - 1) + 1)
        pl.semaphore_signal(barrier, inc=1, device_id={"frame": to}, device_id_type=MESH)

    act[pl.ds(0, width), :] = jnp.zeros((width, 3 * channels), BF16)
    act[pl.ds((height + 1) * width, width), :] = jnp.zeros((width, 3 * channels), BF16)

    per_group = channels // GROUPS
    lanes = lax.broadcasted_iota(jnp.int32, (8, channels), 1)
    column = lax.broadcasted_iota(jnp.int32, (width, channels), 0)

    def group_mean(values):
        total = jnp.broadcast_to(values, (8, channels))
        step = 1
        while step < per_group:
            total = total + jnp.where(
                (lanes // step) % 2 == 0,
                pltpu.roll(total, channels - step, 1),
                pltpu.roll(total, step, 1),
            )
            step *= 2
        return total[:1] * (1.0 / per_group)

    def fold(v):
        return jnp.sum(v.reshape(width // 8, 8, channels), axis=0)

    def moments(shift, s1, s2):
        m1 = group_mean(jnp.sum(s1, axis=0, keepdims=True) * (1.0 / pixels))
        m2 = group_mean(jnp.sum(s2, axis=0, keepdims=True) * (1.0 / pixels))
        return shift + m1, lax.rsqrt(jnp.maximum(m2 - m1 * m1, 0.0) + EPSILON)

    def row_of(i):
        return pl.ds(i * width if isinstance(i, int) else pl.multiple_of(i * width, width), width)

    def activate(value, mean, inv, gain):
        half = inv * gain * 0.5
        @pl.loop(0, height)
        def _(i):
            v = (value(i) - mean) * half
            y = (v * jnp.tanh(v) + v).astype(BF16)
            wide = y.astype(F32)
            there = pl.ds(pl.multiple_of((i + 1) * width, width), width)
            act[there, pl.ds(0, channels)] = jnp.where(
                column == 0, 0.0, pltpu.roll(wide, 1, 0)
            ).astype(BF16)
            act[there, pl.ds(channels, channels)] = y
            act[there, pl.ds(2 * channels, channels)] = jnp.where(
                column == width - 1, 0.0, pltpu.roll(wide, width - 1, 0)
            ).astype(BF16)

    def conv(w_ref, start):
        total = None
        for a in range(3):
            term = dot(
                act[pl.ds(start + a * width, width), :],
                w_ref[pl.ds(a * 3 * channels, 3 * channels), :],
            )
            total = term if total is None else total + term
        return total

    def sums(value, shift, s1, s2):
        d = value - shift
        return s1 + fold(d), s2 + fold(d * d)

    def forward(f, k, to, source, start, low, high):
        return pltpu.make_async_remote_copy(
            src_ref=local.at[f, pl.ds(start, (high - low) * UNIT)],
            dst_ref=recv.at[source * per + f, pl.ds(low * UNIT, (high - low) * UNIT)],
            send_sem=send1.at[f],
            recv_sem=recv1.at[f + k],
            device_id={"frame": to},
            device_id_type=MESH,
        )

    def everything(ref, sem):
        pltpu.make_async_copy(ref, ref, sem).wait()

    def ship(f, part, r, c):
        for k, low, high in pieces(f, c):
            if k == part:
                start = pl.multiple_of(r * width + (first[c] + low) * UNIT, UNIT)
                forward(f, k, owner(r, c), me, start, low, high).start()

    zero = jnp.zeros((8, channels), F32)

    for f in range(per):
        if f == 0:
            loads[0].wait()
            loads[1].wait()
        else:
            loads[4 + f].wait()

        def pixels_of(i):
            return x_ref[f, row_of(i), :].astype(F32)

        shift = group_mean(pixels_of(0)[:1])
        s1, s2 = zero, zero
        for i in range(height):
            s1, s2 = sums(pixels_of(i), shift, s1, s2)
        activate(pixels_of, *moments(shift, s1, s2), g1_ref[...])

        if f == 0:
            loads[2].wait()
        shift, s1, s2 = None, zero, zero
        for i in range(height):
            value = conv(w1_ref, i * width)
            hid[row_of(i), :] = value
            if shift is None:
                shift = group_mean(value[:1])
            s1, s2 = sums(value, shift, s1, s2)
        if f == 0:
            loads[3].wait()
        activate(lambda i: hid[row_of(i), :], *moments(shift, s1, s2), g2_ref[...])

        if f == 0:
            loads[4].wait()
        for i, r in enumerate(order):
            base = pl.multiple_of(r * width, width)
            there = pl.ds(base, width)
            local[f, there, :] = (x_ref[f, there, :].astype(F32) + conv(w2_ref, base)).astype(BF16)
            if f == 0 and i == 0:
                pl.semaphore_wait(barrier, n - 1)
            for c in range(owners):
                if i < height - 1:
                    ship(f, 0, r, c)
                elif counts[c]:
                    pl.when(c != own_share)(functools.partial(ship, f, 0, r, c))

                    @pl.when(c == own_share)
                    def _():
                        size = counts[c] * UNIT
                        recv[me * per + f, pl.ds(0, size), :] = local[
                            f, pl.ds(pl.multiple_of(base + first[c] * UNIT, UNIT), size), :
                        ]

        for k in range(1, parts if f == per - 1 else 1):
            for i, r in enumerate(order):
                for c in range(owners):
                    if i < height - 1:
                        ship(f, k, r, c)
                    else:
                        pl.when(c != own_share)(functools.partial(ship, f, k, r, c))

    for copy in loads[4 + per :]:
        copy.wait()

    lane = lax.broadcasted_iota(jnp.int32, (1, channels), 1) // (channels // heads)
    ri = lax.broadcasted_iota(jnp.int32, (block, rows), 0) % SUB
    rj = lax.broadcasted_iota(jnp.int32, (block, rows), 1) % SUB
    same_pixel = ri == rj

    def count_of(device):
        c = share_of(device)
        return ((c + 1) * units) // owners - (c * units) // owners

    def unit_rows(device, u, size=1):
        c = share_of(device)
        start = (device // owners) * units + (c * units) // owners + u
        return pl.ds(pl.multiple_of(start * UNIT, UNIT), size * UNIT)

    def returning(q, size, to, source):
        return pltpu.make_async_remote_copy(
            src_ref=fin.at[q, to, :, pl.ds(0, size * UNIT)],
            dst_ref=out_ref.at[:, unit_rows(source, batches[q][0], size)],
            send_sem=send2.at[q],
            recv_sem=recv2,
            device_id={"frame": to},
            device_id_type=MESH,
        )

    def attend(q, u):
        x = recv[:, pl.ds(pl.multiple_of(u * UNIT, UNIT), UNIT), :]
        x = x.astype(F32).reshape(frames * UNIT, channels)
        c = x - jnp.mean(x, axis=-1, keepdims=True)
        var = jnp.mean(c * c, axis=-1, keepdims=True)
        normed = (c * lax.rsqrt(var + EPSILON) * pn_ref[...]).astype(BF16)
        for ref, w in ((q_s, wq_ref), (k_s, wk_ref), (v_s, wv_ref)):
            t = dot(normed, w[...]).reshape(frames, UNIT, channels)
            for half in range(halves):
                ref[half] = (
                    t[:, half * SUB : (half + 1) * SUB].reshape(rows, channels).astype(BF16)
                )

        @pl.loop(0, halves)
        def _(half):
            @pl.loop(0, rows // block)
            def _(b):
                qs = pl.ds(pl.multiple_of(b * block, block), block)
                q = q_s[half, qs, :]
                k = k_s[half]
                v = v_s[half]
                total = None
                for h in range(heads):
                    mask = jnp.where(lane == h, 1.0, 0.0).astype(BF16)
                    s = lax.dot_general(
                        q * mask, k, (((1,), (1,)), ((), ())), preferred_element_type=F32
                    )
                    s = s * (sharp_ref[h] * (1.0 / math.sqrt(channels // heads)))
                    s = jnp.where(same_pixel, s, -jnp.inf)
                    e = jnp.exp(s - jnp.max(s, axis=-1, keepdims=True))
                    p = (e * (1.0 / jnp.sum(e, axis=-1, keepdims=True))).astype(BF16)
                    term = dot(p, v * mask)
                    total = term if total is None else total + term
                o_s[half, qs, :] = total

        attended = jnp.concatenate(
            [o_s[half].reshape(frames, SUB, channels) for half in range(halves)], axis=1
        )
        attended = attended.reshape(frames * UNIT, channels).astype(BF16)
        x = recv[:, pl.ds(pl.multiple_of(u * UNIT, UNIT), UNIT), :]
        x = x.astype(F32).reshape(frames * UNIT, channels)
        mixed = (x + dot(attended, wo_ref[...])).astype(BF16)
        edge = jnp.zeros((UNIT, channels), BF16)
        before = jnp.concatenate([edge, mixed[:-UNIT]], axis=0)
        after = jnp.concatenate([mixed[UNIT:], edge], axis=0)
        result = mixed.astype(F32)
        for t, m in enumerate((before, mixed, after)):
            result = result + dot(m, tt_ref[t])
        place = pl.ds(pl.multiple_of((u - batches[q][0]) * UNIT, UNIT), UNIT)
        fin[q, :, :, place, :] = result.astype(BF16).reshape(n, per, UNIT, channels)

    def give(q, size):
        for i, r in enumerate(order):
            for c in range(owners):

                def send():
                    returning(q, size, r * owners + c, me).start()

                if i < height - 1:
                    send()
                else:
                    pl.when(c != seat)(send)
        out_ref[:, unit_rows(me, batches[q][0], size), :] = fin[q, me, :, pl.ds(0, size * UNIT), :]

    cuts = cut(most)
    sizes = sorted(set(counts))
    mine = count_of(me)
    for k in range(parts):
        for size in sizes:
            if cuts[k] >= size:
                continue
            c = counts.index(size)

            @pl.when(mine == size)
            def _():
                for f in range(per):
                    for piece, low, high in pieces(f, c):
                        if piece == k:
                            arrived = recv.at[pl.ds(0, n - 1), pl.ds(0, (high - low) * UNIT)]
                            everything(arrived, recv1.at[f + k])

        for q, (low, high) in enumerate(batches):
            if not cuts[k] <= low < cuts[k + 1]:
                continue

            @pl.loop(low, high)
            def _(u):
                @pl.when(u < mine)
                def _():
                    attend(q, u)

            for size in sizes:
                if low < size:
                    pl.when(mine == size)(functools.partial(give, q, min(high, size) - low))

    for size in sizes:

        @pl.when(mine == size)
        def _():
            others = pl.ds(0, pixels - size * UNIT)
            for f in range(per):
                everything(local.at[f, others], send1.at[f])
            for q, (low, high) in enumerate(batches):
                if low < size:
                    sent = pl.ds(0, (min(high, size) - low) * UNIT)
                    everything(fin.at[q, pl.ds(0, n - 1), :, sent], send2.at[q])
            everything(out_ref.at[:, others], recv2)


def on_device(n, latent, g1, w1, g2, w2, pn, wq, wk, wv, wo, tt, sharp):
    per, height, width, channels = latent.shape
    pixels = height * width
    frames = n * per
    heads = sharp.shape[0]
    rows = frames * SUB
    halves = UNIT // SUB
    most = max(shares(width, n // height)[1])
    cuts = cut(most)
    batches = list(zip(cuts[:-1], cuts[1:]))
    hbm = pl.BlockSpec(memory_space=pl.ANY)
    out = pl.pallas_call(
        functools.partial(kernel, n, per, height, width, heads, batches),
        out_shape=pltpu.VMEM((per, pixels, channels), BF16),
        in_specs=[hbm] * 12,
        out_specs=pl.BlockSpec(memory_space=pltpu.VMEM),
        scratch_shapes=[
            pltpu.VMEM((per, pixels, channels), BF16),
            pltpu.VMEM((1, channels), F32),
            pltpu.VMEM((9 * channels, channels), BF16),
            pltpu.VMEM((1, channels), F32),
            pltpu.VMEM((9 * channels, channels), BF16),
            pltpu.VMEM((1, channels), F32),
            pltpu.VMEM(wq.shape, BF16),
            pltpu.VMEM(wk.shape, BF16),
            pltpu.VMEM(wv.shape, BF16),
            pltpu.VMEM(wo.shape, BF16),
            pltpu.VMEM(tt.shape, BF16),
            pltpu.SMEM(sharp.shape, F32),
            pltpu.VMEM(((height + 2) * width, 3 * channels), BF16),
            pltpu.VMEM((pixels, channels), F32),
            pltpu.VMEM((per, pixels, channels), BF16),
            pltpu.VMEM((frames, most * UNIT, channels), BF16),
            pltpu.VMEM((halves, rows, channels), BF16),
            pltpu.VMEM((halves, rows, channels), BF16),
            pltpu.VMEM((halves, rows, channels), BF16),
            pltpu.VMEM((halves, rows, channels), F32),
            pltpu.VMEM((len(batches), n, per, max(b - a for a, b in batches) * UNIT, channels), BF16),
            pltpu.SemaphoreType.DMA((per + 11,)),
            pltpu.SemaphoreType.DMA((per,)),
            pltpu.SemaphoreType.DMA((per + len(batches) - 1,)),
            pltpu.SemaphoreType.DMA((len(batches),)),
            pltpu.SemaphoreType.DMA,
        ],
        compiler_params=pltpu.CompilerParams(
            collective_id=0, has_side_effects=True, vmem_limit_bytes=58 * 1024 * 1024
        ),
        name="block",
    )(
        latent.reshape(per, pixels, channels),
        g1.reshape(1, channels),
        w1.reshape(9 * channels, channels),
        g2.reshape(1, channels),
        w2.reshape(9 * channels, channels),
        pn.reshape(1, channels),
        wq,
        wk,
        wv,
        wo,
        tt,
        sharp,
    )
    return out.reshape(latent.shape)


def solution(mesh):
    split = P(("groups", "frame"), None, None, None)
    return jax.shard_map(
        functools.partial(on_device, mesh.shape["frame"]),
        mesh=mesh,
        in_specs=(split,) + (P(),) * 11,
        out_specs=split,
        check_vma=False,
    )
```

```python
import functools
import math

import jax
import jax.numpy as jnp
from jax import lax
from jax.experimental import pallas as pl
from jax.experimental.pallas import tpu as pltpu
from jax.sharding import PartitionSpec as P

GROUPS = 32
EPSILON = 1e-05
SUB = 8
UNIT = 16
F32 = jnp.float32
BF16 = jnp.bfloat16
MESH = pl.DeviceIdType.MESH


def dot(a, b):
    return jnp.dot(a, b, preferred_element_type=F32)


def shares(width, owners):
    units = width // UNIT
    first = [c * units // owners for c in range(owners + 1)]
    return first, [first[c + 1] - first[c] for c in range(owners)]


def cut(most):
    return [*range(max(most - 1, 1)), most]


def kernel(
    n,
    per,
    height,
    width,
    heads,
    batches,
    x_hbm,
    g1_hbm,
    w1_hbm,
    g2_hbm,
    w2_hbm,
    pn_hbm,
    wq_hbm,
    wk_hbm,
    wv_hbm,
    wo_hbm,
    tt_hbm,
    sharp_hbm,
    out_ref,
    x_ref,
    g1_ref,
    w1_ref,
    g2_ref,
    w2_ref,
    pn_ref,
    wq_ref,
    wk_ref,
    wv_ref,
    wo_ref,
    tt_ref,
    sharp_ref,
    act,
    hid,
    local,
    recv,
    q_s,
    k_s,
    v_s,
    o_s,
    fin,
    load,
    send1,
    recv1,
    send2,
    recv2,
):
    me = lax.axis_index("frame")
    pixels = height * width
    channels = x_ref.shape[-1]
    frames = n * per
    owners = n // height
    units = width // UNIT
    first, counts = shares(width, owners)
    most = max(counts)
    parts = len(batches)
    rows = frames * SUB
    block = min(rows, 256)
    halves = UNIT // SUB
    plane = me // owners
    seat = me % owners

    def owner(r, c):
        return r * owners + lax.rem(c + owners // 2 * lax.rem(r, 2), owners)

    def share_of(device):
        return lax.rem(device + owners - owners // 2 * lax.rem(device // owners, 2), owners)

    own_share = share_of(me)
    order = [
        height - 1 - plane,
        lax.rem(plane + height // 2, height),
        plane + 1 - 2 * lax.rem(plane, 2),
        plane,
    ]

    def pieces(f, c):
        cuts = cut(most) if f == per - 1 else [0, most]
        return [
            (k, cuts[k], min(cuts[k + 1], counts[c]))
            for k in range(len(cuts) - 1)
            if cuts[k] < counts[c]
        ]

    def peer(j):
        return lax.rem(me + j, n), lax.rem(me + n - j, n)

    loads = []
    for source, target in (
        (x_hbm.at[0], x_ref.at[0]),
        (g1_hbm, g1_ref),
        (w1_hbm, w1_ref),
        (g2_hbm, g2_ref),
        (w2_hbm, w2_ref),
        *((x_hbm.at[f], x_ref.at[f]) for f in range(1, per)),
        (pn_hbm, pn_ref),
        (wq_hbm, wq_ref),
        (wk_hbm, wk_ref),
        (wv_hbm, wv_ref),
        (wo_hbm, wo_ref),
        (tt_hbm, tt_ref),
        (sharp_hbm, sharp_ref),
    ):
        loads.append(pltpu.make_async_copy(source, target, load.at[len(loads)]))
    for copy in loads[:3]:
        copy.start()

    barrier = pltpu.get_barrier_semaphore()

    @pl.loop(1, n)
    def _(j):
        to, _ = peer(lax.rem(j + n // 2 - 1, n - 1) + 1)
        pl.semaphore_signal(barrier, inc=1, device_id={"frame": to}, device_id_type=MESH)

    for copy in loads[3:]:
        copy.start()

    act[pl.ds(0, width), :] = jnp.zeros((width, 3 * channels), BF16)
    act[pl.ds((height + 1) * width, width), :] = jnp.zeros((width, 3 * channels), BF16)

    per_group = channels // GROUPS
    lanes = lax.broadcasted_iota(jnp.int32, (8, channels), 1)
    column = lax.broadcasted_iota(jnp.int32, (width, channels), 0)

    def group_mean(values):
        total = jnp.broadcast_to(values, (8, channels))
        step = 1
        while step < per_group:
            total = total + jnp.where(
                (lanes // step) % 2 == 0,
                pltpu.roll(total, channels - step, 1),
                pltpu.roll(total, step, 1),
            )
            step *= 2
        return total[:1] * (1.0 / per_group)

    def fold(v):
        return jnp.sum(v.reshape(width // 8, 8, channels), axis=0)

    def moments(shift, s1, s2):
        m1 = group_mean(jnp.sum(s1, axis=0, keepdims=True) * (1.0 / pixels))
        m2 = group_mean(jnp.sum(s2, axis=0, keepdims=True) * (1.0 / pixels))
        return shift + m1, lax.rsqrt(jnp.maximum(m2 - m1 * m1, 0.0) + EPSILON)

    def row_of(i):
        return pl.ds(i * width if isinstance(i, int) else pl.multiple_of(i * width, width), width)

    def activate(value, mean, inv, gain):
        half = inv * gain * 0.5
        @pl.loop(0, height)
        def _(i):
            v = (value(i) - mean) * half
            y = (v * jnp.tanh(v) + v).astype(BF16)
            wide = y.astype(F32)
            there = pl.ds(pl.multiple_of((i + 1) * width, width), width)
            act[there, pl.ds(0, channels)] = jnp.where(
                column == 0, 0.0, pltpu.roll(wide, 1, 0)
            ).astype(BF16)
            act[there, pl.ds(channels, channels)] = y
            act[there, pl.ds(2 * channels, channels)] = jnp.where(
                column == width - 1, 0.0, pltpu.roll(wide, width - 1, 0)
            ).astype(BF16)

    def conv(w_ref, start):
        total = None
        for a in range(3):
            term = dot(
                act[pl.ds(start + a * width, width), :],
                w_ref[pl.ds(a * 3 * channels, 3 * channels), :],
            )
            total = term if total is None else total + term
        return total

    def sums(value, shift, s1, s2):
        d = value - shift
        return s1 + fold(d), s2 + fold(d * d)

    def forward(f, k, to, source, start, low, high):
        return pltpu.make_async_remote_copy(
            src_ref=local.at[f, pl.ds(start, (high - low) * UNIT)],
            dst_ref=recv.at[source * per + f, pl.ds(low * UNIT, (high - low) * UNIT)],
            send_sem=send1.at[f],
            recv_sem=recv1.at[f + k],
            device_id={"frame": to},
            device_id_type=MESH,
        )

    def everything(ref, sem):
        pltpu.make_async_copy(ref, ref, sem).wait()

    def ship(f, part, r, c):
        for k, low, high in pieces(f, c):
            if k == part:
                start = pl.multiple_of(r * width + (first[c] + low) * UNIT, UNIT)
                forward(f, k, owner(r, c), me, start, low, high).start()

    zero = jnp.zeros((8, channels), F32)

    for f in range(per):
        if f == 0:
            loads[0].wait()
            loads[1].wait()
        else:
            loads[4 + f].wait()

        def pixels_of(i):
            return x_ref[f, row_of(i), :].astype(F32)

        shift = group_mean(pixels_of(0)[:1])
        s1, s2 = lax.fori_loop(
            0, height, lambda i, carry: sums(pixels_of(i), shift, *carry), (zero, zero)
        )
        activate(pixels_of, *moments(shift, s1, s2), g1_ref[...])

        if f == 0:
            loads[2].wait()
        shift, s1, s2 = None, zero, zero
        for i in range(height):
            value = conv(w1_ref, i * width)
            hid[row_of(i), :] = value
            if shift is None:
                shift = group_mean(value[:1])
            s1, s2 = sums(value, shift, s1, s2)
        if f == 0:
            loads[3].wait()
        activate(lambda i: hid[row_of(i), :], *moments(shift, s1, s2), g2_ref[...])

        if f == 0:
            loads[4].wait()
        for i, r in enumerate(order):
            base = pl.multiple_of(r * width, width)
            there = pl.ds(base, width)
            local[f, there, :] = (x_ref[f, there, :].astype(F32) + conv(w2_ref, base)).astype(BF16)
            if f == 0 and i == 0:
                pl.semaphore_wait(barrier, n - 1)
            for c in range(owners):
                if i < height - 1:
                    ship(f, 0, r, c)
                elif counts[c]:
                    pl.when(c != own_share)(functools.partial(ship, f, 0, r, c))

                    @pl.when(c == own_share)
                    def _():
                        size = counts[c] * UNIT
                        recv[me * per + f, pl.ds(0, size), :] = local[
                            f, pl.ds(pl.multiple_of(base + first[c] * UNIT, UNIT), size), :
                        ]

        for k in range(1, parts if f == per - 1 else 1):
            for i, r in enumerate(order):
                for c in range(owners):
                    if i < height - 1:
                        ship(f, k, r, c)
                    else:
                        pl.when(c != own_share)(functools.partial(ship, f, k, r, c))

    for copy in loads[4 + per :]:
        copy.wait()

    lane = lax.broadcasted_iota(jnp.int32, (1, channels), 1) // (channels // heads)
    ri = lax.broadcasted_iota(jnp.int32, (block, rows), 0) % SUB
    rj = lax.broadcasted_iota(jnp.int32, (block, rows), 1) % SUB
    same_pixel = ri == rj

    def count_of(device):
        c = share_of(device)
        return ((c + 1) * units) // owners - (c * units) // owners

    def unit_rows(device, u, size=1):
        c = share_of(device)
        start = (device // owners) * units + (c * units) // owners + u
        return pl.ds(pl.multiple_of(start * UNIT, UNIT), size * UNIT)

    def returning(q, size, to, source):
        return pltpu.make_async_remote_copy(
            src_ref=fin.at[q, to, :, pl.ds(0, size * UNIT)],
            dst_ref=out_ref.at[:, unit_rows(source, batches[q][0], size)],
            send_sem=send2.at[q],
            recv_sem=recv2,
            device_id={"frame": to},
            device_id_type=MESH,
        )

    def attend(q, u):
        x = recv[:, pl.ds(pl.multiple_of(u * UNIT, UNIT), UNIT), :]
        x = x.astype(F32).reshape(frames * UNIT, channels)
        c = x - jnp.mean(x, axis=-1, keepdims=True)
        var = jnp.mean(c * c, axis=-1, keepdims=True)
        normed = (c * lax.rsqrt(var + EPSILON) * pn_ref[...]).astype(BF16)
        for ref, w in ((q_s, wq_ref), (k_s, wk_ref), (v_s, wv_ref)):
            t = dot(normed, w[...]).reshape(frames, UNIT, channels)
            for half in range(halves):
                ref[half] = (
                    t[:, half * SUB : (half + 1) * SUB].reshape(rows, channels).astype(BF16)
                )

        @pl.loop(0, halves)
        def _(half):
            @pl.loop(0, rows // block)
            def _(b):
                qs = pl.ds(pl.multiple_of(b * block, block), block)
                q = q_s[half, qs, :]
                k = k_s[half]
                v = v_s[half]
                total = None
                for h in range(heads):
                    mask = jnp.where(lane == h, 1.0, 0.0).astype(BF16)
                    s = lax.dot_general(
                        q * mask, k, (((1,), (1,)), ((), ())), preferred_element_type=F32
                    )
                    s = s * (sharp_ref[h] * (1.0 / math.sqrt(channels // heads)))
                    s = jnp.where(same_pixel, s, -jnp.inf)
                    e = jnp.exp(s - jnp.max(s, axis=-1, keepdims=True))
                    p = (e * (1.0 / jnp.sum(e, axis=-1, keepdims=True))).astype(BF16)
                    term = dot(p, v * mask)
                    total = term if total is None else total + term
                o_s[half, qs, :] = total

        attended = jnp.concatenate(
            [o_s[half].reshape(frames, SUB, channels) for half in range(halves)], axis=1
        )
        attended = attended.reshape(frames * UNIT, channels).astype(BF16)
        x = recv[:, pl.ds(pl.multiple_of(u * UNIT, UNIT), UNIT), :]
        x = x.astype(F32).reshape(frames * UNIT, channels)
        mixed = (x + dot(attended, wo_ref[...])).astype(BF16)
        edge = jnp.zeros((UNIT, channels), BF16)
        before = jnp.concatenate([edge, mixed[:-UNIT]], axis=0)
        after = jnp.concatenate([mixed[UNIT:], edge], axis=0)
        result = mixed.astype(F32)
        for t, m in enumerate((before, mixed, after)):
            result = result + dot(m, tt_ref[t])
        place = pl.ds(pl.multiple_of((u - batches[q][0]) * UNIT, UNIT), UNIT)
        fin[q, :, :, place, :] = result.astype(BF16).reshape(n, per, UNIT, channels)

    def give(q, size):
        for i, r in enumerate(order):
            for c in range(owners):

                def send():
                    returning(q, size, r * owners + c, me).start()

                if i < height - 1:
                    send()
                else:
                    pl.when(c != seat)(send)
        out_ref[:, unit_rows(me, batches[q][0], size), :] = fin[q, me, :, pl.ds(0, size * UNIT), :]

    cuts = cut(most)
    sizes = sorted(set(counts))
    mine = count_of(me)
    for k in range(parts):
        for size in sizes:
            if cuts[k] >= size:
                continue
            c = counts.index(size)

            @pl.when(mine == size)
            def _():
                for f in range(per):
                    for piece, low, high in pieces(f, c):
                        if piece == k:
                            arrived = recv.at[pl.ds(0, n - 1), pl.ds(0, (high - low) * UNIT)]
                            everything(arrived, recv1.at[f + k])

        for q, (low, high) in enumerate(batches):
            if not cuts[k] <= low < cuts[k + 1]:
                continue

            @pl.loop(low, high)
            def _(u):
                @pl.when(u < mine)
                def _():
                    attend(q, u)

            for size in sizes:
                if low < size:
                    pl.when(mine == size)(functools.partial(give, q, min(high, size) - low))

    for size in sizes:

        @pl.when(mine == size)
        def _():
            others = pl.ds(0, pixels - size * UNIT)
            for f in range(per):
                everything(local.at[f, others], send1.at[f])
            for q, (low, high) in enumerate(batches):
                if low < size:
                    sent = pl.ds(0, (min(high, size) - low) * UNIT)
                    everything(fin.at[q, pl.ds(0, n - 1), :, sent], send2.at[q])
            everything(out_ref.at[:, others], recv2)


def on_device(n, latent, g1, w1, g2, w2, pn, wq, wk, wv, wo, tt, sharp):
    per, height, width, channels = latent.shape
    pixels = height * width
    frames = n * per
    heads = sharp.shape[0]
    rows = frames * SUB
    halves = UNIT // SUB
    most = max(shares(width, n // height)[1])
    cuts = cut(most)
    batches = list(zip(cuts[:-1], cuts[1:]))
    hbm = pl.BlockSpec(memory_space=pl.ANY)
    out = pl.pallas_call(
        functools.partial(kernel, n, per, height, width, heads, batches),
        out_shape=pltpu.VMEM((per, pixels, channels), BF16),
        in_specs=[hbm] * 12,
        out_specs=pl.BlockSpec(memory_space=pltpu.VMEM),
        scratch_shapes=[
            pltpu.VMEM((per, pixels, channels), BF16),
            pltpu.VMEM((1, channels), F32),
            pltpu.VMEM((9 * channels, channels), BF16),
            pltpu.VMEM((1, channels), F32),
            pltpu.VMEM((9 * channels, channels), BF16),
            pltpu.VMEM((1, channels), F32),
            pltpu.VMEM(wq.shape, BF16),
            pltpu.VMEM(wk.shape, BF16),
            pltpu.VMEM(wv.shape, BF16),
            pltpu.VMEM(wo.shape, BF16),
            pltpu.VMEM(tt.shape, BF16),
            pltpu.SMEM(sharp.shape, F32),
            pltpu.VMEM(((height + 2) * width, 3 * channels), BF16),
            pltpu.VMEM((pixels, channels), F32),
            pltpu.VMEM((per, pixels, channels), BF16),
            pltpu.VMEM((frames, most * UNIT, channels), BF16),
            pltpu.VMEM((halves, rows, channels), BF16),
            pltpu.VMEM((halves, rows, channels), BF16),
            pltpu.VMEM((halves, rows, channels), BF16),
            pltpu.VMEM((halves, rows, channels), F32),
            pltpu.VMEM((len(batches), n, per, max(b - a for a, b in batches) * UNIT, channels), BF16),
            pltpu.SemaphoreType.DMA((per + 11,)),
            pltpu.SemaphoreType.DMA((per,)),
            pltpu.SemaphoreType.DMA((per + len(batches) - 1,)),
            pltpu.SemaphoreType.DMA((len(batches),)),
            pltpu.SemaphoreType.DMA,
        ],
        compiler_params=pltpu.CompilerParams(
            collective_id=0, has_side_effects=True, vmem_limit_bytes=58 * 1024 * 1024
        ),
        name="block",
    )(
        latent.reshape(per, pixels, channels),
        g1.reshape(1, channels),
        w1.reshape(9 * channels, channels),
        g2.reshape(1, channels),
        w2.reshape(9 * channels, channels),
        pn.reshape(1, channels),
        wq,
        wk,
        wv,
        wo,
        tt,
        sharp,
    )
    return out.reshape(latent.shape)


def solution(mesh):
    split = P(("groups", "frame"), None, None, None)
    return jax.shard_map(
        functools.partial(on_device, mesh.shape["frame"]),
        mesh=mesh,
        in_specs=(split,) + (P(),) * 11,
        out_specs=split,
        check_vma=False,
    )
```

```python
import functools
import math

import jax
import jax.numpy as jnp
from jax import lax
from jax.experimental import pallas as pl
from jax.experimental.pallas import tpu as pltpu
from jax.sharding import PartitionSpec as P

GROUPS = 32
EPSILON = 1e-05
SUB = 8
UNIT = 16
F32 = jnp.float32
BF16 = jnp.bfloat16
MESH = pl.DeviceIdType.MESH


def dot(a, b):
    return jnp.dot(a, b, preferred_element_type=F32)


def shares(width, owners):
    units = width // UNIT
    first = [c * units // owners for c in range(owners + 1)]
    return first, [first[c + 1] - first[c] for c in range(owners)]


def cut(most):
    return [*range(max(most - 1, 1)), most]


def kernel(
    n,
    per,
    height,
    width,
    heads,
    batches,
    x_hbm,
    g1_hbm,
    w1_hbm,
    g2_hbm,
    w2_hbm,
    pn_hbm,
    wq_hbm,
    wk_hbm,
    wv_hbm,
    wo_hbm,
    tt_hbm,
    sharp_hbm,
    out_ref,
    x_ref,
    g1_ref,
    w1_ref,
    g2_ref,
    w2_ref,
    pn_ref,
    wq_ref,
    wk_ref,
    wv_ref,
    wo_ref,
    tt_ref,
    sharp_ref,
    act,
    hid,
    local,
    recv,
    q_s,
    k_s,
    v_s,
    o_s,
    fin,
    load,
    send1,
    recv1,
    send2,
    recv2,
):
    me = lax.axis_index("frame")
    pixels = height * width
    channels = x_ref.shape[-1]
    frames = n * per
    owners = n // height
    units = width // UNIT
    first, counts = shares(width, owners)
    most = max(counts)
    parts = len(batches)
    rows = frames * SUB
    block = min(rows, 256)
    halves = UNIT // SUB
    plane = me // owners
    seat = me % owners

    def owner(r, c):
        return r * owners + lax.rem(c + owners // 2 * lax.rem(r, 2), owners)

    def share_of(device):
        return lax.rem(device + owners - owners // 2 * lax.rem(device // owners, 2), owners)

    own_share = share_of(me)
    order = [
        height - 1 - plane,
        lax.rem(plane + height // 2, height),
        plane + 1 - 2 * lax.rem(plane, 2),
        plane,
    ]

    def pieces(f, c):
        cuts = cut(most) if f == per - 1 else [0, most]
        return [
            (k, cuts[k], min(cuts[k + 1], counts[c]))
            for k in range(len(cuts) - 1)
            if cuts[k] < counts[c]
        ]

    def peer(j):
        return lax.rem(me + j, n), lax.rem(me + n - j, n)

    loads = []
    for source, target in (
        (x_hbm.at[0], x_ref.at[0]),
        (g1_hbm, g1_ref),
        (w1_hbm, w1_ref),
        (g2_hbm, g2_ref),
        (w2_hbm, w2_ref),
        *((x_hbm.at[f], x_ref.at[f]) for f in range(1, per)),
        (pn_hbm, pn_ref),
        (wq_hbm, wq_ref),
        (wk_hbm, wk_ref),
        (wv_hbm, wv_ref),
        (wo_hbm, wo_ref),
        (tt_hbm, tt_ref),
        (sharp_hbm, sharp_ref),
    ):
        loads.append(pltpu.make_async_copy(source, target, load.at[len(loads)]))
    for copy in loads[:3]:
        copy.start()

    barrier = pltpu.get_barrier_semaphore()

    @pl.loop(1, n)
    def _(j):
        to, _ = peer(lax.rem(j + n // 2 - 1, n - 1) + 1)
        pl.semaphore_signal(barrier, inc=1, device_id={"frame": to}, device_id_type=MESH)

    for copy in loads[3:]:
        copy.start()

    act[pl.ds(0, width), :] = jnp.zeros((width, 3 * channels), BF16)
    act[pl.ds((height + 1) * width, width), :] = jnp.zeros((width, 3 * channels), BF16)

    per_group = channels // GROUPS
    lanes = lax.broadcasted_iota(jnp.int32, (8, channels), 1)
    column = lax.broadcasted_iota(jnp.int32, (width, channels), 0)

    def group_mean(values):
        total = jnp.broadcast_to(values, (8, channels))
        step = 1
        while step < per_group:
            total = total + jnp.where(
                (lanes // step) % 2 == 0,
                pltpu.roll(total, channels - step, 1),
                pltpu.roll(total, step, 1),
            )
            step *= 2
        return total[:1] * (1.0 / per_group)

    def fold(v):
        return jnp.sum(v.reshape(width // 8, 8, channels), axis=0)

    def moments(shift, s1, s2):
        m1 = group_mean(jnp.sum(s1, axis=0, keepdims=True) * (1.0 / pixels))
        m2 = group_mean(jnp.sum(s2, axis=0, keepdims=True) * (1.0 / pixels))
        return shift + m1, lax.rsqrt(jnp.maximum(m2 - m1 * m1, 0.0) + EPSILON)

    def row_of(i):
        return pl.ds(i * width if isinstance(i, int) else pl.multiple_of(i * width, width), width)

    def activate(value, mean, inv, gain):
        half = inv * gain * 0.5
        @pl.loop(0, height)
        def _(i):
            v = (value(i) - mean) * half
            y = (v * jnp.tanh(v) + v).astype(BF16)
            wide = y.astype(F32)
            there = pl.ds(pl.multiple_of((i + 1) * width, width), width)
            act[there, pl.ds(0, channels)] = jnp.where(
                column == 0, 0.0, pltpu.roll(wide, 1, 0)
            ).astype(BF16)
            act[there, pl.ds(channels, channels)] = y
            act[there, pl.ds(2 * channels, channels)] = jnp.where(
                column == width - 1, 0.0, pltpu.roll(wide, width - 1, 0)
            ).astype(BF16)

    def conv(w_ref, start, size=width):
        total = None
        for a in range(3):
            term = dot(
                act[pl.ds(start + a * width, size), :],
                w_ref[pl.ds(a * 3 * channels, 3 * channels), :],
            )
            total = term if total is None else total + term
        return total

    def sums(value, shift, s1, s2):
        d = value - shift
        return s1 + fold(d), s2 + fold(d * d)

    def forward(f, k, to, source, start, low, high):
        return pltpu.make_async_remote_copy(
            src_ref=local.at[f, pl.ds(start, (high - low) * UNIT)],
            dst_ref=recv.at[source * per + f, pl.ds(low * UNIT, (high - low) * UNIT)],
            send_sem=send1.at[f],
            recv_sem=recv1.at[f + k],
            device_id={"frame": to},
            device_id_type=MESH,
        )

    def everything(ref, sem):
        pltpu.make_async_copy(ref, ref, sem).wait()

    def ship(f, part, r, c):
        for k, low, high in pieces(f, c):
            if k == part:
                start = pl.multiple_of(r * width + (first[c] + low) * UNIT, UNIT)
                forward(f, k, owner(r, c), me, start, low, high).start()

    zero = jnp.zeros((8, channels), F32)

    for f in range(per):
        if f == 0:
            loads[0].wait()
            loads[1].wait()
        else:
            loads[4 + f].wait()

        def pixels_of(i):
            return x_ref[f, row_of(i), :].astype(F32)

        shift = group_mean(pixels_of(0)[:1])
        s1, s2 = lax.fori_loop(
            0, height, lambda i, carry: sums(pixels_of(i), shift, *carry), (zero, zero)
        )
        activate(pixels_of, *moments(shift, s1, s2), g1_ref[...])

        if f == 0:
            loads[2].wait()
        shift, s1, s2 = None, zero, zero
        for i in range(height):
            value = conv(w1_ref, i * width)
            hid[row_of(i), :] = value
            if shift is None:
                shift = group_mean(value[:1])
            s1, s2 = sums(value, shift, s1, s2)
        if f == 0:
            loads[3].wait()
        activate(lambda i: hid[row_of(i), :], *moments(shift, s1, s2), g2_ref[...])

        if f == 0:
            loads[4].wait()
        for i, r in enumerate(order):
            base = pl.multiple_of(r * width, width)
            middle = owners // 2
            spans = [(0, middle), (middle, owners)] if f == 0 and i == 0 else [(0, owners)]
            for low, high in spans:
                begin = first[low] * UNIT
                size = (first[high] if high < owners else units) * UNIT - begin
                start = pl.multiple_of(base + begin, UNIT)
                there = pl.ds(start, size)
                local[f, there, :] = (
                    x_ref[f, there, :].astype(F32) + conv(w2_ref, start, size)
                ).astype(BF16)
                if f == 0 and i == 0 and low == 0:
                    pl.semaphore_wait(barrier, n - 1)
                for c in range(low, high):
                    if i < height - 1:
                        ship(f, 0, r, c)
                    elif counts[c]:
                        pl.when(c != own_share)(functools.partial(ship, f, 0, r, c))

                        @pl.when(c == own_share)
                        def _():
                            size = counts[c] * UNIT
                            recv[me * per + f, pl.ds(0, size), :] = local[
                                f, pl.ds(pl.multiple_of(base + first[c] * UNIT, UNIT), size), :
                            ]

        for k in range(1, parts if f == per - 1 else 1):
            for i, r in enumerate(order):
                for c in range(owners):
                    if i < height - 1:
                        ship(f, k, r, c)
                    else:
                        pl.when(c != own_share)(functools.partial(ship, f, k, r, c))

    for copy in loads[4 + per :]:
        copy.wait()

    lane = lax.broadcasted_iota(jnp.int32, (1, channels), 1) // (channels // heads)
    ri = lax.broadcasted_iota(jnp.int32, (block, rows), 0) % SUB
    rj = lax.broadcasted_iota(jnp.int32, (block, rows), 1) % SUB
    same_pixel = ri == rj

    def count_of(device):
        c = share_of(device)
        return ((c + 1) * units) // owners - (c * units) // owners

    def unit_rows(device, u, size=1):
        c = share_of(device)
        start = (device // owners) * units + (c * units) // owners + u
        return pl.ds(pl.multiple_of(start * UNIT, UNIT), size * UNIT)

    def returning(q, size, to, source):
        return pltpu.make_async_remote_copy(
            src_ref=fin.at[q, to, :, pl.ds(0, size * UNIT)],
            dst_ref=out_ref.at[:, unit_rows(source, batches[q][0], size)],
            send_sem=send2.at[q],
            recv_sem=recv2,
            device_id={"frame": to},
            device_id_type=MESH,
        )

    def attend(q, u):
        x = recv[:, pl.ds(pl.multiple_of(u * UNIT, UNIT), UNIT), :]
        x = x.astype(F32).reshape(frames * UNIT, channels)
        c = x - jnp.mean(x, axis=-1, keepdims=True)
        var = jnp.mean(c * c, axis=-1, keepdims=True)
        normed = (c * lax.rsqrt(var + EPSILON) * pn_ref[...]).astype(BF16)
        for ref, w in ((q_s, wq_ref), (k_s, wk_ref), (v_s, wv_ref)):
            t = dot(normed, w[...]).reshape(frames, UNIT, channels)
            for half in range(halves):
                ref[half] = (
                    t[:, half * SUB : (half + 1) * SUB].reshape(rows, channels).astype(BF16)
                )

        @pl.loop(0, halves)
        def _(half):
            @pl.loop(0, rows // block)
            def _(b):
                qs = pl.ds(pl.multiple_of(b * block, block), block)
                q = q_s[half, qs, :]
                k = k_s[half]
                v = v_s[half]
                total = None
                for h in range(heads):
                    mask = jnp.where(lane == h, 1.0, 0.0).astype(BF16)
                    s = lax.dot_general(
                        q * mask, k, (((1,), (1,)), ((), ())), preferred_element_type=F32
                    )
                    s = s * (sharp_ref[h] * (1.0 / math.sqrt(channels // heads)))
                    s = jnp.where(same_pixel, s, -jnp.inf)
                    e = jnp.exp(s - jnp.max(s, axis=-1, keepdims=True))
                    p = (e * (1.0 / jnp.sum(e, axis=-1, keepdims=True))).astype(BF16)
                    term = dot(p, v * mask)
                    total = term if total is None else total + term
                o_s[half, qs, :] = total

        attended = jnp.concatenate(
            [o_s[half].reshape(frames, SUB, channels) for half in range(halves)], axis=1
        )
        attended = attended.reshape(frames * UNIT, channels).astype(BF16)
        x = recv[:, pl.ds(pl.multiple_of(u * UNIT, UNIT), UNIT), :]
        x = x.astype(F32).reshape(frames * UNIT, channels)
        mixed = (x + dot(attended, wo_ref[...])).astype(BF16)
        edge = jnp.zeros((UNIT, channels), BF16)
        before = jnp.concatenate([edge, mixed[:-UNIT]], axis=0)
        after = jnp.concatenate([mixed[UNIT:], edge], axis=0)
        result = mixed.astype(F32)
        for t, m in enumerate((before, mixed, after)):
            result = result + dot(m, tt_ref[t])
        place = pl.ds(pl.multiple_of((u - batches[q][0]) * UNIT, UNIT), UNIT)
        fin[q, :, :, place, :] = result.astype(BF16).reshape(n, per, UNIT, channels)

    def give(q, size):
        for i, r in enumerate(order):
            for c in range(owners):

                def send():
                    returning(q, size, r * owners + c, me).start()

                if i < height - 1:
                    send()
                else:
                    pl.when(c != seat)(send)
        out_ref[:, unit_rows(me, batches[q][0], size), :] = fin[q, me, :, pl.ds(0, size * UNIT), :]

    cuts = cut(most)
    sizes = sorted(set(counts))
    mine = count_of(me)
    for k in range(parts):
        for size in sizes:
            if cuts[k] >= size:
                continue
            c = counts.index(size)

            @pl.when(mine == size)
            def _():
                for f in range(per):
                    for piece, low, high in pieces(f, c):
                        if piece == k:
                            arrived = recv.at[pl.ds(0, n - 1), pl.ds(0, (high - low) * UNIT)]
                            everything(arrived, recv1.at[f + k])

        for q, (low, high) in enumerate(batches):
            if not cuts[k] <= low < cuts[k + 1]:
                continue

            @pl.loop(low, high)
            def _(u):
                @pl.when(u < mine)
                def _():
                    attend(q, u)

            for size in sizes:
                if low < size:
                    pl.when(mine == size)(functools.partial(give, q, min(high, size) - low))

    for size in sizes:

        @pl.when(mine == size)
        def _():
            others = pl.ds(0, pixels - size * UNIT)
            for f in range(per):
                everything(local.at[f, others], send1.at[f])
            for q, (low, high) in enumerate(batches):
                if low < size:
                    sent = pl.ds(0, (min(high, size) - low) * UNIT)
                    everything(fin.at[q, pl.ds(0, n - 1), :, sent], send2.at[q])
            everything(out_ref.at[:, others], recv2)


def on_device(n, latent, g1, w1, g2, w2, pn, wq, wk, wv, wo, tt, sharp):
    per, height, width, channels = latent.shape
    pixels = height * width
    frames = n * per
    heads = sharp.shape[0]
    rows = frames * SUB
    halves = UNIT // SUB
    most = max(shares(width, n // height)[1])
    cuts = cut(most)
    batches = list(zip(cuts[:-1], cuts[1:]))
    hbm = pl.BlockSpec(memory_space=pl.ANY)
    out = pl.pallas_call(
        functools.partial(kernel, n, per, height, width, heads, batches),
        out_shape=pltpu.VMEM((per, pixels, channels), BF16),
        in_specs=[hbm] * 12,
        out_specs=pl.BlockSpec(memory_space=pltpu.VMEM),
        scratch_shapes=[
            pltpu.VMEM((per, pixels, channels), BF16),
            pltpu.VMEM((1, channels), F32),
            pltpu.VMEM((9 * channels, channels), BF16),
            pltpu.VMEM((1, channels), F32),
            pltpu.VMEM((9 * channels, channels), BF16),
            pltpu.VMEM((1, channels), F32),
            pltpu.VMEM(wq.shape, BF16),
            pltpu.VMEM(wk.shape, BF16),
            pltpu.VMEM(wv.shape, BF16),
            pltpu.VMEM(wo.shape, BF16),
            pltpu.VMEM(tt.shape, BF16),
            pltpu.SMEM(sharp.shape, F32),
            pltpu.VMEM(((height + 2) * width, 3 * channels), BF16),
            pltpu.VMEM((pixels, channels), F32),
            pltpu.VMEM((per, pixels, channels), BF16),
            pltpu.VMEM((frames, most * UNIT, channels), BF16),
            pltpu.VMEM((halves, rows, channels), BF16),
            pltpu.VMEM((halves, rows, channels), BF16),
            pltpu.VMEM((halves, rows, channels), BF16),
            pltpu.VMEM((halves, rows, channels), F32),
            pltpu.VMEM((len(batches), n, per, max(b - a for a, b in batches) * UNIT, channels), BF16),
            pltpu.SemaphoreType.DMA((per + 11,)),
            pltpu.SemaphoreType.DMA((per,)),
            pltpu.SemaphoreType.DMA((per + len(batches) - 1,)),
            pltpu.SemaphoreType.DMA((len(batches),)),
            pltpu.SemaphoreType.DMA,
        ],
        compiler_params=pltpu.CompilerParams(
            collective_id=0, has_side_effects=True, vmem_limit_bytes=58 * 1024 * 1024
        ),
        name="block",
    )(
        latent.reshape(per, pixels, channels),
        g1.reshape(1, channels),
        w1.reshape(9 * channels, channels),
        g2.reshape(1, channels),
        w2.reshape(9 * channels, channels),
        pn.reshape(1, channels),
        wq,
        wk,
        wv,
        wo,
        tt,
        sharp,
    )
    return out.reshape(latent.shape)


def solution(mesh):
    split = P(("groups", "frame"), None, None, None)
    return jax.shard_map(
        functools.partial(on_device, mesh.shape["frame"]),
        mesh=mesh,
        in_specs=(split,) + (P(),) * 11,
        out_specs=split,
        check_vma=False,
    )
```
